128 devices in a mesh: tm: 32 (over z, y, core), space: 4 (over x).
Axes of the slice: x: 4, y: 4, z: 4, core: 2. Of those that a mesh axis runs over, the one named last changes fastest.
Arguments:
- frames_in: bfloat16 [32, 256, 128, 128], P('tm', None, 'space'), may hold values from -6 to 6
- conv_weight: bfloat16 [3, 3, 256, 256], replicated, may hold values from -0.125 to 0.125
- out_weight: bfloat16 [256, 256], replicated, may hold values from -0.375 to 0.375
- skip_gain: float32 [256], replicated, may hold values from -4 to 4
- decays: float32 [32, 256], P('tm'), may hold values from 0.25 to 1, as said below
Outputs:
- frames_out: bfloat16 [32, 256, 128, 128], P('tm', None, 'space')
The draws below stay inside these ranges and needn't reach their ends.
Inputs may be any that keep to these rules, and one draw needn't show every extreme that they name: `decays`: every entry lies strictly below 1.
All inputs are finite; a program needn't handle non-finite values.
Results may differ from the reference program's by a relative error of at most 0.0041.
Values may be sent and summed in bfloat16 or wider, within the bound.
A program may use at most 320 MiB of HBM per device.

```python
import math
import jax
import jax.numpy as jnp
from jax import lax

C = 256
P_SIZE = 256
H = 128
W = 128
SPAN_STEPS = 32


def draw_decays(key, part):
    seed_handles = jax.random.split(key, 6)
    slow_share = 0.5
    slow = jax.random.uniform(seed_handles[0], (P_SIZE,)) < slow_share
    rate_slow = jnp.exp(jax.random.uniform(seed_handles[1], (P_SIZE,), minval=math.log(0.3 / SPAN_STEPS), maxval=math.log(2.0 / SPAN_STEPS)))
    rate_fast = 1.0 / jax.random.uniform(seed_handles[2], (P_SIZE,), minval=10.0, maxval=17.0)
    base = jnp.where(slow, rate_slow, rate_fast)
    rough = jax.random.uniform(seed_handles[3], (SPAN_STEPS, P_SIZE), minval=0.5, maxval=2.0)
    kept = jnp.exp(-base[None, :] * rough)
    spike_instant = jax.random.randint(seed_handles[4], (4,), 0, SPAN_STEPS)
    impacted_steps = jnp.any(jnp.arange(SPAN_STEPS)[:, None] == spike_instant[None, :], axis=1)
    factor = jax.random.uniform(seed_handles[5], (SPAN_STEPS, P_SIZE), minval=0.5, maxval=0.8)
    return jnp.where(impacted_steps[:, None], kept * factor, kept).astype(jnp.float32)


def block_levels(rng, extent, cuts, smallest, largest):
    def one(axis_at, blocks):
        heights = jax.random.uniform(jax.random.fold_in(jax.random.fold_in(rng, 6), axis_at), (blocks,), jnp.float32, smallest / len(cuts), largest / len(cuts))
        return jnp.repeat(jnp.exp(heights), extent[axis_at] // blocks).reshape((-1,) + (1,) * (len(extent) - axis_at - 1))

    gain = one(*cuts[0])
    for cut in cuts[1:]:
        gain = gain * one(*cut)
    return gain


def noise(stream_key, extent, spread, bound, cuts=(), dtype=jnp.bfloat16):
    drawn = spread * jax.random.normal(stream_key, extent, jnp.float32)
    if cuts:
        drawn = drawn * block_levels(stream_key, extent, cuts, -0.22, 0.18)
    return jnp.clip(drawn, -bound, bound).astype(dtype)


def setup_inputs(seed: int = 0) -> dict:
    streams_of = jax.random.split(jax.random.key(seed), 6)
    return {
        "frames_in": noise(streams_of[0], (SPAN_STEPS, C, H, W), 1.0, 6.0, ((0, 32), (2, 4))),
        "conv_weight": noise(streams_of[1], (3, 3, P_SIZE, C), (9 * C) ** -0.5, 0.125),
        "out_weight": noise(streams_of[2], (C, P_SIZE), P_SIZE ** -0.5, 0.375),
        "skip_gain": noise(streams_of[3], (C,), 0.7, 4.0, (), jnp.float32),
        "decays": draw_decays(jax.random.fold_in(streams_of[5], 71), 0),
    }


def reference(frames_in, conv_weight, out_weight, skip_gain, decays):
    conv_f32 = conv_weight.astype(jnp.float32)
    out_f32 = out_weight.astype(jnp.float32)

    def frame_step(memory, frame_data):
        frame_x, frame_decay = frame_data
        frame_f32 = frame_x.astype(jnp.float32)
        padded = jnp.pad(frame_f32, ((0, 0), (1, 1), (1, 1)))
        driving = jnp.zeros((P_SIZE, H, W), jnp.float32)
        for vertical_shift in range(3):
            for col_off in range(3):
                driving = driving + jnp.einsum('pc,chw->phw', conv_f32[vertical_shift, col_off], padded[:, vertical_shift:vertical_shift + H, col_off:col_off + W])
        in_gain = jnp.sqrt(1.0 - frame_decay * frame_decay)
        memory = frame_decay[:, None, None] * memory + in_gain[:, None, None] * driving
        rounded = lax.optimization_barrier(memory.astype(jnp.bfloat16)).astype(jnp.float32)
        output = jnp.einsum('cp,phw->chw', out_f32, rounded) + skip_gain[:, None, None] * frame_f32
        return (memory, output.astype(jnp.bfloat16))
    start = jnp.zeros((P_SIZE, H, W), jnp.float32)
    ending, output_frames = lax.scan(frame_step, start, (frames_in, decays))
    return output_frames
```

```python
import functools

import jax
import jax.numpy as jnp
from jax import lax
from jax.experimental import pallas as pl
from jax.experimental.pallas import tpu as pltpu
from jax.sharding import PartitionSpec as P

MESH = pl.DeviceIdType.MESH
ROWS = 32
HALF = 16
CH = 256
WIDTH = 128
CHIPS = 16
BAND = CH // CHIPS
CHUNKS = 4
STEP = HALF // CHUNKS
F32 = jnp.float32
BF16 = jnp.bfloat16


def column(row):
    return jnp.transpose(jnp.broadcast_to(row, (WIDTH, CH)), (1, 0))


def kernel(
    x_hbm, w_hbm, wo_hbm, skip_ref, dec_ref, y_hbm,
    xp, wc, wo, drive, coef, decs, achip, pair_out, pair_in, merged, up_in, down_out, entry,
    last_out, last_in, y_buf,
    load_sem, store_sem, halo_s, halo_r, dec_s, dec_r, a_s, a_r, pair_s, pair_r, up_s, up_r,
    down_s, down_r, last_s, last_r,
):
    tm = lax.axis_index("tm")
    sp = lax.axis_index("space")
    chip = tm // 2
    core = lax.rem(tm, 2)
    partner = chip * 2 + (1 - core)
    above = lax.rem(sp + 3, 4)
    below = lax.rem(sp + 1, 4)

    def peer(d):
        return lax.rem(chip + d, CHIPS)

    loads = [
        pltpu.make_async_copy(x_hbm, xp.at[pl.ds(1, ROWS)], load_sem.at[0]),
        pltpu.make_async_copy(wo_hbm, wo, load_sem.at[1]),
    ]
    for i in range(3):
        for j in range(3):
            loads.append(
                pltpu.make_async_copy(
                    w_hbm.at[i, j],
                    wc.at[pl.ds(j * CH, CH), pl.ds(i * CH, CH)],
                    load_sem.at[2 + 3 * i + j],
                )
            )
    for load in loads:
        load.start()

    barrier = pltpu.get_barrier_semaphore()

    def greet(d, carry):
        pl.semaphore_signal(
            barrier, inc=1, device_id={"tm": peer(d) * 2 + core}, device_id_type=MESH
        )
        return carry

    pl.semaphore_signal(barrier, inc=1, device_id={"tm": partner}, device_id_type=MESH)
    pl.semaphore_signal(barrier, inc=1, device_id={"space": above}, device_id_type=MESH)
    pl.semaphore_signal(barrier, inc=1, device_id={"space": below}, device_id_type=MESH)
    lax.fori_loop(1, CHIPS, greet, 0)

    own_decay = column(dec_ref[...])
    decs[0] = own_decay
    coef[0] = jnp.sqrt(1.0 - own_decay * own_decay)
    coef[4] = column(skip_ref[...])

    pl.semaphore_wait(barrier, CHIPS + 2)

    def halo(side):
        row, slot, target = ((ROWS - 1, 0, below), (0, ROWS + 1, above))[side]
        return pltpu.make_async_remote_copy(
            src_ref=x_hbm.at[row], dst_ref=xp.at[slot], send_sem=halo_s.at[side],
            recv_sem=halo_r.at[side], device_id={"space": target}, device_id_type=MESH,
        )

    halo(0).start()
    halo(1).start()
    dec_copy = pltpu.make_async_remote_copy(
        src_ref=decs.at[0], dst_ref=decs.at[1], send_sem=dec_s, recv_sem=dec_r,
        device_id={"tm": partner}, device_id_type=MESH,
    )
    dec_copy.start()
    for load in loads:
        load.wait()

    def first_row(s, q):
        return (1 - s) * (HALF - STEP * (q + 1)) + s * (STEP * q)

    lane = lax.broadcasted_iota(jnp.int32, (CH, WIDTH), 1)

    def conv_rows(h):
        view = [xp[h + i] for i in range(4)]
        right = jnp.concatenate(
            [jnp.concatenate([view[i], view[i + 1]], axis=1) for i in range(3)], axis=0
        )
        acc = jnp.dot(wc[...], right, preferred_element_type=F32)
        for e in range(2):
            part = acc[:, e * WIDTH : (e + 1) * WIDTH]
            left = jnp.where(lane == 0, 0.0, pltpu.roll(part[0:CH], 1, 1))
            after = jnp.where(lane == WIDTH - 1, 0.0, pltpu.roll(part[2 * CH :], WIDTH - 1, 1))
            drive[h + e] = coef[0] * (left + part[CH : 2 * CH] + after)

    def pair_copy(q):
        r = first_row(1 - core, q)
        return pltpu.make_async_remote_copy(
            src_ref=pair_out.at[pl.ds(r, STEP)], dst_ref=pair_in.at[pl.ds(r, STEP)],
            send_sem=pair_s.at[q], recv_sem=pair_r.at[q],
            device_id={"tm": partner}, device_id_type=MESH,
        )

    def pair_arrival(q):
        r = first_row(core, q)
        return pltpu.make_async_remote_copy(
            src_ref=pair_out.at[pl.ds(r, STEP)], dst_ref=pair_in.at[pl.ds(r, STEP)],
            send_sem=pair_s.at[q], recv_sem=pair_r.at[q],
            device_id={"tm": partner}, device_id_type=MESH,
        )

    def a_copy(d):
        to = peer(d)
        return pltpu.make_async_remote_copy(
            src_ref=coef.at[5, pl.ds(pl.multiple_of(to * BAND, BAND), BAND)],
            dst_ref=achip.at[chip],
            send_sem=a_s.at[d], recv_sem=a_r.at[d],
            device_id={"tm": to * 2 + core}, device_id_type=MESH,
        )

    def up_copy(q, d):
        to = peer(d)
        r = first_row(core, q)
        return pltpu.make_async_remote_copy(
            src_ref=merged.at[pl.ds(r, STEP), pl.ds(pl.multiple_of(to * BAND, BAND), BAND)],
            dst_ref=up_in.at[chip, pl.ds(r, STEP)],
            send_sem=up_s.at[q, d], recv_sem=up_r.at[q, d],
            device_id={"tm": to * 2 + core}, device_id_type=MESH,
        )

    def up_local(q):
        r = first_row(core, q)
        return pltpu.make_async_copy(
            merged.at[pl.ds(r, STEP), pl.ds(pl.multiple_of(chip * BAND, BAND), BAND)],
            up_in.at[chip, pl.ds(r, STEP)],
            up_s.at[q, 0],
        )

    def down_copy(q, d):
        to = peer(d)
        r = first_row(core, q)
        return pltpu.make_async_remote_copy(
            src_ref=down_out.at[to, pl.ds(r, STEP)],
            dst_ref=entry.at[pl.ds(r, STEP), pl.ds(pl.multiple_of(chip * BAND, BAND), BAND)],
            send_sem=down_s.at[q, d], recv_sem=down_r.at[q, d],
            device_id={"tm": to * 2 + core}, device_id_type=MESH,
        )

    def down_local(q):
        r = first_row(core, q)
        return pltpu.make_async_copy(
            down_out.at[chip, pl.ds(r, STEP)],
            entry.at[pl.ds(r, STEP), pl.ds(pl.multiple_of(chip * BAND, BAND), BAND)],
            down_s.at[q, 0],
        )

    def last_copy(q):
        r = first_row(core, q)
        return pltpu.make_async_remote_copy(
            src_ref=last_out.at[pl.ds(r, STEP)], dst_ref=last_in.at[pl.ds(r, STEP)],
            send_sem=last_s.at[q], recv_sem=last_r.at[q],
            device_id={"tm": partner}, device_id_type=MESH,
        )

    def last_arrival(q):
        r = first_row(1 - core, q)
        return pltpu.make_async_remote_copy(
            src_ref=last_out.at[pl.ds(r, STEP)], dst_ref=last_in.at[pl.ds(r, STEP)],
            send_sem=last_s.at[q], recv_sem=last_r.at[q],
            device_id={"tm": partner}, device_id_type=MESH,
        )

    def each(n0, n1, body):
        def run(i, carry):
            body(i)
            return carry

        lax.fori_loop(n0, n1, run, 0)

    other = 1 - core

    def send_half(q):
        @pl.when(q == CHUNKS - 1)
        def _():
            halo(0).wait()
            halo(1).wait()

            @pl.when(sp == 0)
            def _():
                xp[0] = jnp.zeros((CH, WIDTH), BF16)

            @pl.when(sp == 3)
            def _():
                xp[ROWS + 1] = jnp.zeros((CH, WIDTH), BF16)

        r0 = first_row(other, q)

        def tile(t):
            r = r0 + 2 * t
            conv_rows(r + HALF * other)
            for e in range(2):
                pair_out[r + e] = drive[r + HALF * other + e].astype(BF16)

        each(0, STEP // 2, tile)
        pair_copy(q).start()

    each(0, CHUNKS, send_half)

    dec_copy.wait()
    mine = decs[0]
    theirs = decs[1]
    second = core.astype(F32)
    coef[1] = (1.0 - second) * theirs + second
    coef[2] = (1.0 - second) + second * mine
    coef[5] = mine * theirs
    coef[3] = (1.0 - second) * mine + second * (mine * theirs)
    each(1, CHIPS, lambda d: a_copy(d).start())
    a_local = pltpu.make_async_copy(
        coef.at[5, pl.ds(pl.multiple_of(chip * BAND, BAND), BAND)], achip.at[chip], a_s.at[0]
    )
    a_local.start()

    def merge_half(q):
        r0 = first_row(core, q)

        def tile(t):
            conv_rows(r0 + 2 * t + HALF * core)

        each(0, STEP // 2, tile)
        pair_arrival(q).wait_recv()

        def merge(e):
            r = r0 + e
            own = drive[r + HALF * core]
            total = coef[1] * own + coef[2] * pair_in[r].astype(F32)
            merged[r] = total.astype(BF16)
            drive[r + HALF * core] = (1.0 - second) * own + second * total

        each(0, STEP, merge)
        each(1, CHIPS, lambda d: up_copy(q, d).start())
        up_local(q).start()

    each(0, CHUNKS, merge_half)

    each(1, CHIPS, lambda d: a_copy(d).wait())
    a_local.wait()

    def scan(q):
        each(1, CHIPS, lambda d: up_copy(q, d).wait_recv())
        up_local(q).wait()
        rows = pl.ds(first_row(core, q), STEP)
        state = jnp.zeros((STEP, BAND, WIDTH), F32)
        for i in range(CHIPS):
            down_out[i, rows] = state.astype(BF16)
            if i < CHIPS - 1:
                state = achip[i][None] * state + up_in[i, rows].astype(F32)
        each(1, CHIPS, lambda d: down_copy(q, d).start())
        down_local(q).start()

    each(0, CHUNKS, scan)

    def project(h, memory):
        out = jnp.dot(
            wo[...], jnp.concatenate(memory, axis=1), preferred_element_type=F32
        )
        for e in range(2):
            y_buf[h + e] = (
                out[:, e * WIDTH : (e + 1) * WIDTH] + coef[4] * xp[h + e + 1].astype(F32)
            ).astype(BF16)

    def y_copy(s, q, slot):
        h = first_row(s, q) + HALF * s
        return pltpu.make_async_copy(
            y_buf.at[pl.ds(h, STEP)], y_hbm.at[pl.ds(h, STEP)], store_sem.at[slot, q]
        )

    def finish(q):
        @pl.when(q < CHUNKS)
        def _():
            each(1, CHIPS, lambda d: down_copy(q, d).wait_recv())
            down_local(q).wait()
            r0 = first_row(core, q)

            def answer(e):
                r = r0 + e
                enter = entry[r].astype(F32)
                memory = coef[3] * enter + drive[r + HALF * core]
                drive[r + HALF * core] = memory
                last_out[r] = ((1.0 - second) * memory + second * enter).astype(BF16)

            each(0, STEP, answer)
            last_copy(q).start()

            def tile(t):
                h = r0 + 2 * t + HALF * core
                project(h, [drive[h + e].astype(BF16) for e in range(2)])

            each(0, STEP // 2, tile)
            y_copy(core, q, 0).start()

        @pl.when(q > 0)
        def _():
            p = q - 1
            last_arrival(p).wait_recv()
            r0 = first_row(other, p)

            def tile(t):
                r = r0 + 2 * t
                h = r + HALF * other
                project(
                    h,
                    [
                        (decs[0] * last_in[r + e].astype(F32) + drive[h + e]).astype(BF16)
                        for e in range(2)
                    ],
                )

            each(0, STEP // 2, tile)
            y_copy(other, p, 1).start()

    each(0, CHUNKS + 1, finish)

    def drain(q):
        pair_copy(q).wait_send()
        last_copy(q).wait_send()

        def one(d):
            up_copy(q, d).wait_send()
            down_copy(q, d).wait_send()

        each(1, CHIPS, one)
        y_copy(core, q, 0).wait()
        y_copy(other, q, 1).wait()

    each(0, CHUNKS, drain)


def on_device(frames_in, conv_weight, out_weight, skip_gain, decays):
    rows = jnp.transpose(frames_in[0], (1, 0, 2))
    dma = pltpu.SemaphoreType.DMA
    y = pl.pallas_call(
        kernel,
        out_shape=jax.ShapeDtypeStruct((ROWS, CH, WIDTH), BF16),
        in_specs=[
            pl.BlockSpec(memory_space=pl.ANY),
            pl.BlockSpec(memory_space=pl.ANY),
            pl.BlockSpec(memory_space=pl.ANY),
            pl.BlockSpec(memory_space=pltpu.VMEM),
            pl.BlockSpec(memory_space=pltpu.VMEM),
        ],
        out_specs=pl.BlockSpec(memory_space=pl.ANY),
        scratch_shapes=[
            pltpu.VMEM((ROWS + 2, CH, WIDTH), BF16),
            pltpu.VMEM((3 * CH, 3 * CH), BF16),
            pltpu.VMEM((CH, CH), BF16),
            pltpu.VMEM((ROWS, CH, WIDTH), F32),
            pltpu.VMEM((6, CH, WIDTH), F32),
            pltpu.VMEM((2, CH, WIDTH), F32),
            pltpu.VMEM((CHIPS, BAND, WIDTH), F32),
            pltpu.VMEM((HALF, CH, WIDTH), BF16),
            pltpu.VMEM((HALF, CH, WIDTH), BF16),
            pltpu.VMEM((HALF, CH, WIDTH), BF16),
            pltpu.VMEM((CHIPS, HALF, BAND, WIDTH), BF16),
            pltpu.VMEM((CHIPS, HALF, BAND, WIDTH), BF16),
            pltpu.VMEM((HALF, CH, WIDTH), BF16),
            pltpu.VMEM((HALF, CH, WIDTH), BF16),
            pltpu.VMEM((HALF, CH, WIDTH), BF16),
            pltpu.VMEM((ROWS, CH, WIDTH), BF16),
            dma((11,)),
            dma((2, CHUNKS)),
            dma((2,)),
            dma((2,)),
            dma,
            dma,
            dma((CHIPS,)),
            dma((CHIPS,)),
            dma((CHUNKS,)),
            dma((CHUNKS,)),
            dma((CHUNKS, CHIPS)),
            dma((CHUNKS, CHIPS)),
            dma((CHUNKS, CHIPS)),
            dma((CHUNKS, CHIPS)),
            dma((CHUNKS,)),
            dma((CHUNKS,)),
        ],
        compiler_params=pltpu.CompilerParams(
            collective_id=0, has_side_effects=True, vmem_limit_bytes=48 << 20
        ),
    )(rows, conv_weight, out_weight, skip_gain[None, :], decays)
    return jnp.transpose(y, (1, 0, 2))[None]


def solution(mesh):
    placed = (P("tm", None, "space", None), P(), P(), P(), P("tm", None))
    return jax.shard_map(
        on_device,
        mesh=mesh,
        in_specs=placed,
        out_specs=P("tm", None, "space", None),
        check_vma=False,
    )
```

```python
import functools

import jax
import jax.numpy as jnp
from jax import lax
from jax.experimental import pallas as pl
from jax.experimental.pallas import tpu as pltpu
from jax.sharding import PartitionSpec as P

MESH = pl.DeviceIdType.MESH
ROWS = 32
HALF = 16
CH = 256
WIDTH = 128
CHIPS = 16
BAND = CH // CHIPS
CHUNKS = 4
LAG = 3
STEP = HALF // CHUNKS
F32 = jnp.float32
BF16 = jnp.bfloat16


def column(row):
    return jnp.transpose(jnp.broadcast_to(row, (WIDTH, CH)), (1, 0))


def kernel(
    x_hbm, w_hbm, wo_hbm, skip_ref, dec_ref, y_hbm,
    xp, wc, wo, drive, coef, decs, achip, pair_out, pair_in, merged, up_in, down_out, entry,
    last_out, last_in, y_buf,
    load_sem, store_sem, halo_s, halo_r, dec_s, dec_r, a_s, a_r, pair_s, pair_r, up_s, up_r,
    down_s, down_r, last_s, last_r,
):
    tm = lax.axis_index("tm")
    sp = lax.axis_index("space")
    chip = tm // 2
    core = lax.rem(tm, 2)
    partner = chip * 2 + (1 - core)
    above = lax.rem(sp + 3, 4)
    below = lax.rem(sp + 1, 4)

    def peer(d):
        return lax.rem(chip + d, CHIPS)

    loads = [
        pltpu.make_async_copy(x_hbm, xp.at[pl.ds(1, ROWS)], load_sem.at[0]),
        pltpu.make_async_copy(wo_hbm, wo, load_sem.at[1]),
    ]
    for i in range(3):
        for j in range(3):
            loads.append(
                pltpu.make_async_copy(
                    w_hbm.at[i, j],
                    wc.at[pl.ds(j * CH, CH), pl.ds(i * CH, CH)],
                    load_sem.at[2 + 3 * i + j],
                )
            )
    for load in loads:
        load.start()

    barrier = pltpu.get_barrier_semaphore()

    def greet(d, carry):
        pl.semaphore_signal(
            barrier, inc=1, device_id={"tm": peer(d) * 2 + core}, device_id_type=MESH
        )
        return carry

    pl.semaphore_signal(barrier, inc=1, device_id={"tm": partner}, device_id_type=MESH)
    pl.semaphore_signal(barrier, inc=1, device_id={"space": above}, device_id_type=MESH)
    pl.semaphore_signal(barrier, inc=1, device_id={"space": below}, device_id_type=MESH)
    lax.fori_loop(1, CHIPS, greet, 0)

    own_decay = column(dec_ref[...])
    decs[0] = own_decay
    coef[0] = jnp.sqrt(1.0 - own_decay * own_decay)
    coef[4] = column(skip_ref[...])

    def halo(side):
        row, slot, target = ((ROWS - 1, 0, below), (0, ROWS + 1, above))[side]
        return pltpu.make_async_remote_copy(
            src_ref=x_hbm.at[row], dst_ref=xp.at[slot], send_sem=halo_s.at[side],
            recv_sem=halo_r.at[side], device_id={"space": target}, device_id_type=MESH,
        )

    dec_copy = pltpu.make_async_remote_copy(
        src_ref=decs.at[0], dst_ref=decs.at[1], send_sem=dec_s, recv_sem=dec_r,
        device_id={"tm": partner}, device_id_type=MESH,
    )

    def first_row(s, q):
        return (1 - s) * (HALF - STEP * (q + 1)) + s * (STEP * q)

    lane = lax.broadcasted_iota(jnp.int32, (CH, WIDTH), 1)

    def convolved(h):
        view = [xp[h + i] for i in range(4)]
        right = jnp.concatenate(
            [jnp.concatenate([view[i], view[i + 1]], axis=1) for i in range(3)], axis=0
        )
        return jnp.dot(wc[...], right, preferred_element_type=F32)

    def driven(acc, e):
        part = acc[:, e * WIDTH : (e + 1) * WIDTH]
        left = jnp.where(lane == 0, 0.0, pltpu.roll(part[0:CH], 1, 1))
        after = jnp.where(lane == WIDTH - 1, 0.0, pltpu.roll(part[2 * CH :], WIDTH - 1, 1))
        return coef[0] * (left + part[CH : 2 * CH] + after)

    def pair_copy(q):
        r = first_row(1 - core, q)
        return pltpu.make_async_remote_copy(
            src_ref=pair_out.at[pl.ds(r, STEP)], dst_ref=pair_in.at[pl.ds(r, STEP)],
            send_sem=pair_s.at[q], recv_sem=pair_r.at[q],
            device_id={"tm": partner}, device_id_type=MESH,
        )

    def pair_arrival(q):
        r = first_row(core, q)
        return pltpu.make_async_remote_copy(
            src_ref=pair_out.at[pl.ds(r, STEP)], dst_ref=pair_in.at[pl.ds(r, STEP)],
            send_sem=pair_s.at[q], recv_sem=pair_r.at[q],
            device_id={"tm": partner}, device_id_type=MESH,
        )

    def a_copy(d):
        to = peer(d)
        return pltpu.make_async_remote_copy(
            src_ref=coef.at[5, pl.ds(pl.multiple_of(to * BAND, BAND), BAND)],
            dst_ref=achip.at[chip],
            send_sem=a_s.at[d], recv_sem=a_r.at[d],
            device_id={"tm": to * 2 + core}, device_id_type=MESH,
        )

    def up_copy(q, d):
        to = peer(d)
        r = first_row(core, q)
        return pltpu.make_async_remote_copy(
            src_ref=merged.at[pl.ds(r, STEP), pl.ds(pl.multiple_of(to * BAND, BAND), BAND)],
            dst_ref=up_in.at[chip, pl.ds(r, STEP)],
            send_sem=up_s.at[q, d], recv_sem=up_r.at[q, d],
            device_id={"tm": to * 2 + core}, device_id_type=MESH,
        )

    def up_local(q):
        r = first_row(core, q)
        return pltpu.make_async_copy(
            merged.at[pl.ds(r, STEP), pl.ds(pl.multiple_of(chip * BAND, BAND), BAND)],
            up_in.at[chip, pl.ds(r, STEP)],
            up_s.at[q, 0],
        )

    def down_copy(q, d):
        to = peer(d)
        r = first_row(core, q)
        return pltpu.make_async_remote_copy(
            src_ref=down_out.at[to, pl.ds(r, STEP)],
            dst_ref=entry.at[pl.ds(r, STEP), pl.ds(pl.multiple_of(chip * BAND, BAND), BAND)],
            send_sem=down_s.at[q, d], recv_sem=down_r.at[q, d],
            device_id={"tm": to * 2 + core}, device_id_type=MESH,
        )

    def down_local(q):
        r = first_row(core, q)
        return pltpu.make_async_copy(
            down_out.at[chip, pl.ds(r, STEP)],
            entry.at[pl.ds(r, STEP), pl.ds(pl.multiple_of(chip * BAND, BAND), BAND)],
            down_s.at[q, 0],
        )

    def last_copy(q):
        r = first_row(core, q)
        return pltpu.make_async_remote_copy(
            src_ref=last_out.at[pl.ds(r, STEP)], dst_ref=last_in.at[pl.ds(r, STEP)],
            send_sem=last_s.at[q], recv_sem=last_r.at[q],
            device_id={"tm": partner}, device_id_type=MESH,
        )

    def last_arrival(q):
        r = first_row(1 - core, q)
        return pltpu.make_async_remote_copy(
            src_ref=last_out.at[pl.ds(r, STEP)], dst_ref=last_in.at[pl.ds(r, STEP)],
            send_sem=last_s.at[q], recv_sem=last_r.at[q],
            device_id={"tm": partner}, device_id_type=MESH,
        )

    def each(n0, n1, body):
        def run(i, carry):
            body(i)
            return carry

        lax.fori_loop(n0, n1, run, 0)

    other = 1 - core
    second = core.astype(F32)

    def conv(q):
        r0 = first_row(other, q)
        r1 = first_row(core, q)

        def tile(t):
            r = r0 + 2 * t
            theirs = convolved(r + HALF * other)
            h = r1 + 2 * t + HALF * core
            ours = convolved(h)
            for e in range(2):
                value = driven(theirs, e)
                drive[r + HALF * other + e] = value
                pair_out[r + e] = value.astype(BF16)
            for e in range(2):
                drive[h + e] = driven(ours, e)

        each(0, STEP // 2, tile)

    a_local = pltpu.make_async_copy(
        coef.at[5, pl.ds(pl.multiple_of(chip * BAND, BAND), BAND)], achip.at[chip], a_s.at[0]
    )

    def coefficients():
        dec_copy.wait()
        mine = decs[0]
        theirs = decs[1]
        coef[1] = (1.0 - second) * theirs + second
        coef[2] = (1.0 - second) + second * mine
        coef[5] = mine * theirs
        coef[3] = (1.0 - second) * mine + second * (mine * theirs)
        each(1, CHIPS, lambda d: a_copy(d).start())
        a_local.start()

    def merge_half(q):
        pair_arrival(q).wait_recv()
        r0 = first_row(core, q)

        def merge(e):
            r = r0 + e
            own = drive[r + HALF * core]
            total = coef[1] * own + coef[2] * pair_in[r].astype(F32)
            merged[r] = total.astype(BF16)
            drive[r + HALF * core] = (1.0 - second) * own + second * total

        each(0, STEP, merge)
        each(1, CHIPS, lambda d: up_copy(q, d).start())
        up_local(q).start()

    def scan(q):
        each(1, CHIPS, lambda d: up_copy(q, d).wait_recv())
        up_local(q).wait()
        rows = pl.ds(first_row(core, q), STEP)
        state = jnp.zeros((STEP, BAND, WIDTH), F32)
        for i in range(CHIPS):
            down_out[i, rows] = state.astype(BF16)
            if i < CHIPS - 1:
                state = achip[i][None] * state + up_in[i, rows].astype(F32)
        each(1, CHIPS, lambda d: down_copy(q, d).start())
        down_local(q).start()

    for load in loads:
        load.wait()
    conv(0)
    pl.semaphore_wait(barrier, CHIPS + 2)
    halo(0).start()
    halo(1).start()
    dec_copy.start()
    pair_copy(0).start()

    def front(q):
        @pl.when(q == CHUNKS - 1)
        def _():
            halo(0).wait()
            halo(1).wait()

            @pl.when(sp == 0)
            def _():
                xp[0] = jnp.zeros((CH, WIDTH), BF16)

            @pl.when(sp == 3)
            def _():
                xp[ROWS + 1] = jnp.zeros((CH, WIDTH), BF16)

        @pl.when(q < CHUNKS)
        def _():
            conv(q)
            pair_copy(q).start()

        @pl.when(q == 1)
        def _():
            coefficients()

        @pl.when(q <= CHUNKS)
        def _():
            merge_half(q - 1)

        @pl.when(q == LAG)
        def _():
            each(1, CHIPS, lambda d: a_copy(d).wait())
            a_local.wait()

        @pl.when(q >= LAG)
        def _():
            scan(q - LAG)

    each(1, CHUNKS + LAG, front)

    def project(h, memory):
        out = jnp.dot(
            wo[...], jnp.concatenate(memory, axis=1), preferred_element_type=F32
        )
        for e in range(2):
            y_buf[h + e] = (
                out[:, e * WIDTH : (e + 1) * WIDTH] + coef[4] * xp[h + e + 1].astype(F32)
            ).astype(BF16)

    def y_copy(s, q, slot):
        h = first_row(s, q) + HALF * s
        return pltpu.make_async_copy(
            y_buf.at[pl.ds(h, STEP)], y_hbm.at[pl.ds(h, STEP)], store_sem.at[slot, q]
        )

    def finish(q):
        @pl.when(q < CHUNKS)
        def _():
            each(1, CHIPS, lambda d: down_copy(q, d).wait_recv())
            down_local(q).wait()
            r0 = first_row(core, q)

            def answer(e):
                r = r0 + e
                enter = entry[r].astype(F32)
                memory = coef[3] * enter + drive[r + HALF * core]
                drive[r + HALF * core] = memory
                last_out[r] = ((1.0 - second) * memory + second * enter).astype(BF16)

            each(0, STEP, answer)
            last_copy(q).start()

            def tile(t):
                h = r0 + 2 * t + HALF * core
                project(h, [drive[h + e].astype(BF16) for e in range(2)])

            each(0, STEP // 2, tile)
            y_copy(core, q, 0).start()

        @pl.when(q > 0)
        def _():
            p = q - 1
            last_arrival(p).wait_recv()
            r0 = first_row(other, p)

            def tile(t):
                r = r0 + 2 * t
                h = r + HALF * other
                project(
                    h,
                    [
                        (decs[0] * last_in[r + e].astype(F32) + drive[h + e]).astype(BF16)
                        for e in range(2)
                    ],
                )

            each(0, STEP // 2, tile)
            y_copy(other, p, 1).start()

    each(0, CHUNKS + 1, finish)

    def drain(q):
        pair_copy(q).wait_send()
        last_copy(q).wait_send()

        def one(d):
            up_copy(q, d).wait_send()
            down_copy(q, d).wait_send()

        each(1, CHIPS, one)
        y_copy(core, q, 0).wait()
        y_copy(other, q, 1).wait()

    each(0, CHUNKS, drain)


def on_device(frames_in, conv_weight, out_weight, skip_gain, decays):
    rows = jnp.transpose(frames_in[0], (1, 0, 2))
    dma = pltpu.SemaphoreType.DMA
    y = pl.pallas_call(
        kernel,
        out_shape=jax.ShapeDtypeStruct((ROWS, CH, WIDTH), BF16),
        in_specs=[
            pl.BlockSpec(memory_space=pl.ANY),
            pl.BlockSpec(memory_space=pl.ANY),
            pl.BlockSpec(memory_space=pl.ANY),
            pl.BlockSpec(memory_space=pltpu.VMEM),
            pl.BlockSpec(memory_space=pltpu.VMEM),
        ],
        out_specs=pl.BlockSpec(memory_space=pl.ANY),
        scratch_shapes=[
            pltpu.VMEM((ROWS + 2, CH, WIDTH), BF16),
            pltpu.VMEM((3 * CH, 3 * CH), BF16),
            pltpu.VMEM((CH, CH), BF16),
            pltpu.VMEM((ROWS, CH, WIDTH), F32),
            pltpu.VMEM((6, CH, WIDTH), F32),
            pltpu.VMEM((2, CH, WIDTH), F32),
            pltpu.VMEM((CHIPS, BAND, WIDTH), F32),
            pltpu.VMEM((HALF, CH, WIDTH), BF16),
            pltpu.VMEM((HALF, CH, WIDTH), BF16),
            pltpu.VMEM((HALF, CH, WIDTH), BF16),
            pltpu.VMEM((CHIPS, HALF, BAND, WIDTH), BF16),
            pltpu.VMEM((CHIPS, HALF, BAND, WIDTH), BF16),
            pltpu.VMEM((HALF, CH, WIDTH), BF16),
            pltpu.VMEM((HALF, CH, WIDTH), BF16),
            pltpu.VMEM((HALF, CH, WIDTH), BF16),
            pltpu.VMEM((ROWS, CH, WIDTH), BF16),
            dma((11,)),
            dma((2, CHUNKS)),
            dma((2,)),
            dma((2,)),
            dma,
            dma,
            dma((CHIPS,)),
            dma((CHIPS,)),
            dma((CHUNKS,)),
            dma((CHUNKS,)),
            dma((CHUNKS, CHIPS)),
            dma((CHUNKS, CHIPS)),
            dma((CHUNKS, CHIPS)),
            dma((CHUNKS, CHIPS)),
            dma((CHUNKS,)),
            dma((CHUNKS,)),
        ],
        compiler_params=pltpu.CompilerParams(
            collective_id=0, has_side_effects=True, vmem_limit_bytes=48 << 20
        ),
    )(rows, conv_weight, out_weight, skip_gain[None, :], decays)
    return jnp.transpose(y, (1, 0, 2))[None]


def solution(mesh):
    placed = (P("tm", None, "space", None), P(), P(), P(), P("tm", None))
    return jax.shard_map(
        on_device,
        mesh=mesh,
        in_specs=placed,
        out_specs=P("tm", None, "space", None),
        check_vma=False,
    )
```

```python
import functools

import jax
import jax.numpy as jnp
from jax import lax
from jax.experimental import pallas as pl
from jax.experimental.pallas import tpu as pltpu
from jax.sharding import PartitionSpec as P

MESH = pl.DeviceIdType.MESH
ROWS = 32
HALF = 16
CH = 256
WIDTH = 128
CHIPS = 16
BAND = CH // CHIPS
CHUNKS = 4
GROUP = 8
EARLY = 0
BLOCKS = 8
VMEM_BYTES = 62 << 20
STEP = HALF // CHUNKS
F32 = jnp.float32
BF16 = jnp.bfloat16


def column(row):
    return jnp.transpose(jnp.broadcast_to(row, (WIDTH, CH)), (1, 0))


def kernel(
    x_hbm, w_hbm, wo_hbm, skip_hbm, dec_hbm, y_hbm,
    xp, wc, wo, drive, coef, decs, achip, pair_out, pair_in, merged, up_in, down_out, entry,
    last_out, last_in, y_buf, y_rows, raw, stage, lines,
    load_sem, store_sem, halo_s, halo_r, dec_s, dec_r, a_s, a_r, pair_s, pair_r, up_s, up_r,
    down_s, down_r, last_s, last_r,
):
    tm = lax.axis_index("tm")
    sp = lax.axis_index("space")
    chip = tm // 2
    core = lax.rem(tm, 2)
    partner = chip * 2 + (1 - core)
    above = lax.rem(sp + 3, 4)
    below = lax.rem(sp + 1, 4)

    def peer(d):
        return lax.rem(chip + d, CHIPS)

    barrier = pltpu.get_barrier_semaphore()

    def greet(d, carry):
        pl.semaphore_signal(
            barrier, inc=1, device_id={"tm": peer(d) * 2 + core}, device_id_type=MESH
        )
        return carry

    pl.semaphore_signal(barrier, inc=1, device_id={"tm": partner}, device_id_type=MESH)
    pl.semaphore_signal(barrier, inc=1, device_id={"space": above}, device_id_type=MESH)
    pl.semaphore_signal(barrier, inc=1, device_id={"space": below}, device_id_type=MESH)
    lax.fori_loop(1, CHIPS, greet, 0)

    x_loads = [
        pltpu.make_async_copy(
            x_hbm.at[:, pl.ds(GROUP * b, GROUP)], raw.at[b], load_sem.at[b]
        )
        for b in range(ROWS // GROUP)
    ]
    small_loads = [
        pltpu.make_async_copy(dec_hbm, lines.at[0], load_sem.at[14]),
        pltpu.make_async_copy(skip_hbm, lines.at[1], load_sem.at[15]),
    ]
    for load in small_loads:
        load.start()
    x_loads[1].start()
    x_loads[2].start()
    loads = []
    for i in range(3):
        for j in range(3):
            loads.append(
                pltpu.make_async_copy(
                    w_hbm.at[i, j],
                    wc.at[pl.ds(j * CH, CH), pl.ds(i * CH, CH)],
                    load_sem.at[5 + 3 * i + j],
                )
            )
    wo_load = pltpu.make_async_copy(wo_hbm, wo, load_sem.at[4])
    for load in loads:
        load.start()
    x_loads[0].start()
    x_loads[3].start()
    wo_load.start()

    for load in small_loads:
        load.wait()
    own_decay = column(lines[0])
    decs[0] = own_decay
    coef[0] = jnp.sqrt(1.0 - own_decay * own_decay)
    coef[4] = column(lines[1])

    def halo(side):
        row, slot, target = ((ROWS, 0, below), (1, ROWS + 1, above))[side]
        return pltpu.make_async_remote_copy(
            src_ref=xp.at[row], dst_ref=xp.at[slot], send_sem=halo_s.at[side],
            recv_sem=halo_r.at[side], device_id={"space": target}, device_id_type=MESH,
        )

    def reorder(b):
        x_loads[b].wait()
        stage[...] = raw[b].astype(F32).reshape(CH * GROUP, WIDTH)

        def row(r):
            xp[1 + GROUP * b + r] = stage[pl.ds(r, CH, stride=GROUP), :].astype(BF16)

        for r in range(GROUP):
            row(r)

    dec_copy = pltpu.make_async_remote_copy(
        src_ref=decs.at[0], dst_ref=decs.at[1], send_sem=dec_s, recv_sem=dec_r,
        device_id={"tm": partner}, device_id_type=MESH,
    )

    def first_row(s, q):
        return (1 - s) * (HALF - STEP * (q + 1)) + s * (STEP * q)

    lane = lax.broadcasted_iota(jnp.int32, (CH, WIDTH), 1)

    def convolved(h):
        view = [xp[h + i] for i in range(4)]
        right = jnp.concatenate(
            [jnp.concatenate([view[i], view[i + 1]], axis=1) for i in range(3)], axis=0
        )
        return jnp.dot(wc[...], right, preferred_element_type=F32)

    def driven(acc, e):
        part = acc[:, e * WIDTH : (e + 1) * WIDTH]
        left = jnp.where(lane == 0, 0.0, pltpu.roll(part[0:CH], 1, 1))
        after = jnp.where(lane == WIDTH - 1, 0.0, pltpu.roll(part[2 * CH :], WIDTH - 1, 1))
        return coef[0] * (left + part[CH : 2 * CH] + after)

    def pair_copy(q):
        r = first_row(1 - core, q)
        return pltpu.make_async_remote_copy(
            src_ref=pair_out.at[pl.ds(r, STEP)], dst_ref=pair_in.at[pl.ds(r, STEP)],
            send_sem=pair_s.at[q], recv_sem=pair_r.at[q],
            device_id={"tm": partner}, device_id_type=MESH,
        )

    def pair_arrival(q):
        r = first_row(core, q)
        return pltpu.make_async_remote_copy(
            src_ref=pair_out.at[pl.ds(r, STEP)], dst_ref=pair_in.at[pl.ds(r, STEP)],
            send_sem=pair_s.at[q], recv_sem=pair_r.at[q],
            device_id={"tm": partner}, device_id_type=MESH,
        )

    def a_copy(d):
        to = peer(d)
        return pltpu.make_async_remote_copy(
            src_ref=coef.at[5, pl.ds(pl.multiple_of(to * BAND, BAND), BAND)],
            dst_ref=achip.at[chip],
            send_sem=a_s.at[d], recv_sem=a_r.at[d],
            device_id={"tm": to * 2 + core}, device_id_type=MESH,
        )

    def up_copy(q, d):
        to = peer(d)
        r = first_row(core, q)
        return pltpu.make_async_remote_copy(
            src_ref=merged.at[pl.ds(r, STEP), pl.ds(pl.multiple_of(to * BAND, BAND), BAND)],
            dst_ref=up_in.at[chip, pl.ds(r, STEP)],
            send_sem=up_s.at[q, d], recv_sem=up_r.at[q, d],
            device_id={"tm": to * 2 + core}, device_id_type=MESH,
        )

    def up_local(q):
        r = first_row(core, q)
        return pltpu.make_async_copy(
            merged.at[pl.ds(r, STEP), pl.ds(pl.multiple_of(chip * BAND, BAND), BAND)],
            up_in.at[chip, pl.ds(r, STEP)],
            up_s.at[q, 0],
        )

    def down_copy(q, d):
        to = peer(d)
        r = first_row(core, q)
        return pltpu.make_async_remote_copy(
            src_ref=down_out.at[to, pl.ds(r, STEP)],
            dst_ref=entry.at[pl.ds(r, STEP), pl.ds(pl.multiple_of(chip * BAND, BAND), BAND)],
            send_sem=down_s.at[q, d], recv_sem=down_r.at[q, d],
            device_id={"tm": to * 2 + core}, device_id_type=MESH,
        )

    def down_local(q):
        r = first_row(core, q)
        return pltpu.make_async_copy(
            down_out.at[chip, pl.ds(r, STEP)],
            entry.at[pl.ds(r, STEP), pl.ds(pl.multiple_of(chip * BAND, BAND), BAND)],
            down_s.at[q, 0],
        )

    def last_copy(q):
        r = first_row(core, q)
        return pltpu.make_async_remote_copy(
            src_ref=last_out.at[pl.ds(r, STEP)], dst_ref=last_in.at[pl.ds(r, STEP)],
            send_sem=last_s.at[q], recv_sem=last_r.at[q],
            device_id={"tm": partner}, device_id_type=MESH,
        )

    def last_arrival(q):
        r = first_row(1 - core, q)
        return pltpu.make_async_remote_copy(
            src_ref=last_out.at[pl.ds(r, STEP)], dst_ref=last_in.at[pl.ds(r, STEP)],
            send_sem=last_s.at[q], recv_sem=last_r.at[q],
            device_id={"tm": partner}, device_id_type=MESH,
        )

    def each(n0, n1, body):
        def run(i, carry):
            body(i)
            return carry

        lax.fori_loop(n0, n1, run, 0)

    other = 1 - core
    second = core.astype(F32)

    def conv_tile(q, t):
        r = first_row(other, q) + 2 * t
        theirs = convolved(r + HALF * other)
        h = first_row(core, q) + 2 * t + HALF * core
        ours = convolved(h)
        for e in range(2):
            value = driven(theirs, e)
            drive[r + HALF * other + e] = value
            pair_out[r + e] = value.astype(BF16)
        for e in range(2):
            drive[h + e] = driven(ours, e)

    a_local = pltpu.make_async_copy(
        coef.at[5, pl.ds(pl.multiple_of(chip * BAND, BAND), BAND)], achip.at[chip], a_s.at[0]
    )

    def coefficients():
        dec_copy.wait()
        mine = decs[0]
        theirs = decs[1]
        coef[1] = (1.0 - second) * theirs + second
        coef[2] = (1.0 - second) + second * mine
        coef[5] = mine * theirs
        coef[3] = (1.0 - second) * mine + second * (mine * theirs)
        each(1, CHIPS, lambda d: a_copy(d).start())
        a_local.start()

    def merge_half(q):
        pair_arrival(q).wait_recv()
        r0 = first_row(core, q)

        def merge(e):
            r = r0 + e
            own = drive[r + HALF * core]
            total = coef[1] * own + coef[2] * pair_in[r].astype(F32)
            merged[r] = total.astype(BF16)
            drive[r + HALF * core] = (1.0 - second) * own + second * total

        each(0, STEP, merge)
        each(1, CHIPS, lambda d: up_copy(q, d).start())
        up_local(q).start()

    def scan(q):
        each(1, CHIPS, lambda d: up_copy(q, d).wait_recv())
        up_local(q).wait()
        rows = pl.ds(first_row(core, q), STEP)
        state = jnp.zeros((STEP, BAND, WIDTH), F32)
        for i in range(CHIPS):
            down_out[i, rows] = state.astype(BF16)
            if i < CHIPS - 1:
                state = achip[i][None] * state + up_in[i, rows].astype(F32)
        each(1, CHIPS, lambda d: down_copy(q, d).start())
        down_local(q).start()

    reorder(1)
    reorder(2)
    for load in loads:
        load.wait()
    each(0, STEP // 2, lambda t: conv_tile(0, t))
    pl.semaphore_wait(barrier, CHIPS + 2)
    pair_copy(0).start()
    dec_copy.start()
    reorder(0)
    reorder(3)
    halo(0).start()
    halo(1).start()
    wo_load.wait()

    def front(q):
        @pl.when(q == CHUNKS - 1)
        def _():
            halo(0).wait()
            halo(1).wait()

            @pl.when(sp == 0)
            def _():
                xp[0] = jnp.zeros((CH, WIDTH), BF16)

            @pl.when(sp == 3)
            def _():
                xp[ROWS + 1] = jnp.zeros((CH, WIDTH), BF16)

        def step(t):
            conv_tile(q, t)

            @pl.when((q == 1) & (t == 0))
            def _():
                coefficients()
                merge_half(0)

        each(0, STEP // 2, step)
        pair_copy(q).start()

        @pl.when(q > 1)
        def _():
            merge_half(q - 1)

    each(1, CHUNKS, front)
    each(1, CHIPS, lambda d: a_copy(d).wait())
    a_local.wait()
    each(0, EARLY, scan)
    merge_half(CHUNKS - 1)
    each(EARLY, CHUNKS, scan)

    def project(h, memory):
        out = jnp.dot(
            wo[...], jnp.concatenate(memory, axis=1), preferred_element_type=F32
        )
        for e in range(2):
            row = h + e
            y_rows[row // GROUP, pl.ds(lax.rem(row, GROUP), CH, stride=GROUP), :] = (
                out[:, e * WIDTH : (e + 1) * WIDTH] + coef[4] * xp[row + 1].astype(F32)
            )

    def y_copy(s, q, slot):
        b = (first_row(s, q) + HALF * s) // GROUP
        return pltpu.make_async_copy(
            y_buf.at[b],
            y_hbm.at[:, pl.ds(pl.multiple_of(b * GROUP, GROUP), GROUP)],
            store_sem.at[slot, q],
        )

    def put(s, q, slot):
        @pl.when(lax.rem(q, GROUP // STEP) == GROUP // STEP - 1)
        def _():
            b = (first_row(s, q) + HALF * s) // GROUP
            y_buf[b] = y_rows[b].reshape(CH, GROUP, WIDTH).astype(BF16)
            y_copy(s, q, slot).start()

    def finish(q):
        pair_copy(q).wait_send()
        each(1, CHIPS, lambda d: up_copy(q, d).wait_send())
        each(1, CHIPS, lambda d: down_copy(q, d).wait_recv())
        down_local(q).wait()
        r0 = first_row(core, q)

        def answer(e):
            r = r0 + e
            enter = entry[r].astype(F32)
            memory = coef[3] * enter + drive[r + HALF * core]
            drive[r + HALF * core] = memory
            last_out[r] = ((1.0 - second) * memory + second * enter).astype(BF16)

        each(0, STEP, answer)
        last_copy(q).start()

        def own_tile(t):
            h = r0 + 2 * t + HALF * core
            project(h, [drive[h + e].astype(BF16) for e in range(2)])

        each(0, STEP // 2, own_tile)
        put(core, q, 0)
        last_arrival(q).wait_recv()
        r1 = first_row(other, q)

        def other_tile(t):
            r = r1 + 2 * t
            h = r + HALF * other
            project(
                h,
                [
                    (decs[0] * last_in[r + e].astype(F32) + drive[h + e]).astype(BF16)
                    for e in range(2)
                ],
            )

        each(0, STEP // 2, other_tile)
        put(other, q, 1)
        last_copy(q).wait_send()
        each(1, CHIPS, lambda d: down_copy(q, d).wait_send())

    each(0, CHUNKS, finish)

    def drain(q):
        @pl.when(lax.rem(q, GROUP // STEP) == GROUP // STEP - 1)
        def _():
            y_copy(core, q, 0).wait()
            y_copy(other, q, 1).wait()

    each(0, CHUNKS, drain)


def settle(y_hbm, out_hbm, block, in_sem, out_sem):
    part = CH // BLOCKS
    fetch = [
        pltpu.make_async_copy(y_hbm.at[pl.ds(part * b, part)], block.at[b], in_sem.at[b])
        for b in range(BLOCKS)
    ]
    store = [
        pltpu.make_async_copy(block.at[b], out_hbm.at[pl.ds(part * b, part)], out_sem.at[b])
        for b in range(BLOCKS)
    ]
    for copy in fetch:
        copy.start()
    for b in range(BLOCKS):
        fetch[b].wait()
        store[b].start()
    for copy in store:
        copy.wait()


def on_device(frames_in, conv_weight, out_weight, skip_gain, decays):
    rows = frames_in[0]
    dma = pltpu.SemaphoreType.DMA
    y = pl.pallas_call(
        kernel,
        out_shape=jax.ShapeDtypeStruct((CH, ROWS, WIDTH), BF16),
        in_specs=[pl.BlockSpec(memory_space=pl.ANY)] * 5,
        out_specs=pl.BlockSpec(memory_space=pl.ANY),
        scratch_shapes=[
            pltpu.VMEM((ROWS + 2, CH, WIDTH), BF16),
            pltpu.VMEM((3 * CH, 3 * CH), BF16),
            pltpu.VMEM((CH, CH), BF16),
            pltpu.VMEM((ROWS, CH, WIDTH), F32),
            pltpu.VMEM((6, CH, WIDTH), F32),
            pltpu.VMEM((2, CH, WIDTH), F32),
            pltpu.VMEM((CHIPS, BAND, WIDTH), F32),
            pltpu.VMEM((HALF, CH, WIDTH), BF16),
            pltpu.VMEM((HALF, CH, WIDTH), BF16),
            pltpu.VMEM((HALF, CH, WIDTH), BF16),
            pltpu.VMEM((CHIPS, HALF, BAND, WIDTH), BF16),
            pltpu.VMEM((CHIPS, HALF, BAND, WIDTH), BF16),
            pltpu.VMEM((HALF, CH, WIDTH), BF16),
            pltpu.VMEM((HALF, CH, WIDTH), BF16),
            pltpu.VMEM((HALF, CH, WIDTH), BF16),
            pltpu.VMEM((ROWS // GROUP, CH, GROUP, WIDTH), BF16),
            pltpu.VMEM((ROWS // GROUP, CH * GROUP, WIDTH), F32),
            pltpu.VMEM((ROWS // GROUP, CH, GROUP, WIDTH), BF16),
            pltpu.VMEM((CH * GROUP, WIDTH), F32),
            pltpu.VMEM((2, 1, CH), F32),
            dma((16,)),
            dma((2, CHUNKS)),
            dma((2,)),
            dma((2,)),
            dma,
            dma,
            dma((CHIPS,)),
            dma((CHIPS,)),
            dma((CHUNKS,)),
            dma((CHUNKS,)),
            dma((CHUNKS, CHIPS)),
            dma((CHUNKS, CHIPS)),
            dma((CHUNKS, CHIPS)),
            dma((CHUNKS, CHIPS)),
            dma((CHUNKS,)),
            dma((CHUNKS,)),
        ],
        compiler_params=pltpu.CompilerParams(
            collective_id=0, has_side_effects=True, vmem_limit_bytes=VMEM_BYTES
        ),
    )(rows, conv_weight, out_weight, skip_gain[None, :], decays)
    settled = pl.pallas_call(
        settle,
        out_shape=jax.ShapeDtypeStruct((CH, ROWS, WIDTH), BF16),
        in_specs=[pl.BlockSpec(memory_space=pl.ANY)],
        out_specs=pl.BlockSpec(memory_space=pl.ANY),
        scratch_shapes=[
            pltpu.VMEM((BLOCKS, CH // BLOCKS, ROWS, WIDTH), BF16),
            dma((BLOCKS,)),
            dma((BLOCKS,)),
        ],
        compiler_params=pltpu.CompilerParams(vmem_limit_bytes=VMEM_BYTES),
    )(y)
    return settled[None]


def solution(mesh):
    placed = (P("tm", None, "space", None), P(), P(), P(), P("tm", None))
    return jax.shard_map(
        on_device,
        mesh=mesh,
        in_specs=placed,
        out_specs=P("tm", None, "space", None),
        check_vma=False,
    )
```

```python
import functools

import jax
import jax.numpy as jnp
from jax import lax
from jax.experimental import pallas as pl
from jax.experimental.pallas import tpu as pltpu
from jax.sharding import PartitionSpec as P

MESH = pl.DeviceIdType.MESH
ROWS = 32
HALF = 16
CH = 256
WIDTH = 128
CHIPS = 16
BAND = CH // CHIPS
CHUNKS = 4
GROUP = 8
EARLY = 0
VMEM_BYTES = 48 << 20
STEP = HALF // CHUNKS
F32 = jnp.float32
BF16 = jnp.bfloat16


def column(row):
    return jnp.transpose(jnp.broadcast_to(row, (WIDTH, CH)), (1, 0))


def kernel(
    x_hbm, w_hbm, wo_hbm, skip_hbm, dec_hbm, y_out,
    xp, wc, wo, drive, coef, decs, achip, pair_out, pair_in, merged, up_in, down_out, entry,
    last_out, last_in, y_rows, raw, stage, lines,
    load_sem, halo_s, halo_r, dec_s, dec_r, a_s, a_r, pair_s, pair_r, up_s, up_r,
    down_s, down_r, last_s, last_r,
):
    tm = lax.axis_index("tm")
    sp = lax.axis_index("space")
    chip = tm // 2
    core = lax.rem(tm, 2)
    partner = chip * 2 + (1 - core)
    above = lax.rem(sp + 3, 4)
    below = lax.rem(sp + 1, 4)

    def peer(d):
        return lax.rem(chip + d, CHIPS)

    barrier = pltpu.get_barrier_semaphore()

    def greet(d, carry):
        pl.semaphore_signal(
            barrier, inc=1, device_id={"tm": peer(d) * 2 + core}, device_id_type=MESH
        )
        return carry

    pl.semaphore_signal(barrier, inc=1, device_id={"tm": partner}, device_id_type=MESH)
    pl.semaphore_signal(barrier, inc=1, device_id={"space": above}, device_id_type=MESH)
    pl.semaphore_signal(barrier, inc=1, device_id={"space": below}, device_id_type=MESH)
    lax.fori_loop(1, CHIPS, greet, 0)

    x_loads = [
        pltpu.make_async_copy(
            x_hbm.at[:, pl.ds(GROUP * b, GROUP)], raw.at[b], load_sem.at[b]
        )
        for b in range(ROWS // GROUP)
    ]
    small_loads = [
        pltpu.make_async_copy(dec_hbm, lines.at[0], load_sem.at[14]),
        pltpu.make_async_copy(skip_hbm, lines.at[1], load_sem.at[15]),
    ]
    for load in small_loads:
        load.start()
    x_loads[1].start()
    x_loads[2].start()
    loads = []
    for i in range(3):
        for j in range(3):
            loads.append(
                pltpu.make_async_copy(
                    w_hbm.at[i, j],
                    wc.at[pl.ds(j * CH, CH), pl.ds(i * CH, CH)],
                    load_sem.at[5 + 3 * i + j],
                )
            )
    wo_load = pltpu.make_async_copy(wo_hbm, wo, load_sem.at[4])
    for load in loads:
        load.start()
    x_loads[0].start()
    x_loads[3].start()
    wo_load.start()

    for load in small_loads:
        load.wait()
    own_decay = column(lines[0])
    decs[0] = own_decay
    coef[0] = jnp.sqrt(1.0 - own_decay * own_decay)
    coef[4] = column(lines[1])

    def halo(side):
        row, slot, target = ((ROWS, 0, below), (1, ROWS + 1, above))[side]
        return pltpu.make_async_remote_copy(
            src_ref=xp.at[row], dst_ref=xp.at[slot], send_sem=halo_s.at[side],
            recv_sem=halo_r.at[side], device_id={"space": target}, device_id_type=MESH,
        )

    def reorder(b):
        x_loads[b].wait()
        stage[...] = raw[b].astype(F32).reshape(CH * GROUP, WIDTH)

        def row(r):
            xp[1 + GROUP * b + r] = stage[pl.ds(r, CH, stride=GROUP), :].astype(BF16)

        for r in range(GROUP):
            row(r)

    dec_copy = pltpu.make_async_remote_copy(
        src_ref=lines.at[0], dst_ref=lines.at[2], send_sem=dec_s, recv_sem=dec_r,
        device_id={"tm": partner}, device_id_type=MESH,
    )

    def first_row(s, q):
        return (1 - s) * (HALF - STEP * (q + 1)) + s * (STEP * q)

    lane = lax.broadcasted_iota(jnp.int32, (CH, WIDTH), 1)

    def convolved(h):
        view = [xp[h + i] for i in range(4)]
        right = jnp.concatenate(
            [jnp.concatenate([view[i], view[i + 1]], axis=1) for i in range(3)], axis=0
        )
        return jnp.dot(wc[...], right, preferred_element_type=F32)

    def driven(acc, e):
        part = acc[:, e * WIDTH : (e + 1) * WIDTH]
        left = jnp.where(lane == 0, 0.0, pltpu.roll(part[0:CH], 1, 1))
        after = jnp.where(lane == WIDTH - 1, 0.0, pltpu.roll(part[2 * CH :], WIDTH - 1, 1))
        return coef[0] * (left + part[CH : 2 * CH] + after)

    def pair_copy(q):
        r = first_row(1 - core, q)
        return pltpu.make_async_remote_copy(
            src_ref=pair_out.at[pl.ds(r, STEP)], dst_ref=pair_in.at[pl.ds(r, STEP)],
            send_sem=pair_s.at[q], recv_sem=pair_r.at[q],
            device_id={"tm": partner}, device_id_type=MESH,
        )

    def pair_arrival(q):
        r = first_row(core, q)
        return pltpu.make_async_remote_copy(
            src_ref=pair_out.at[pl.ds(r, STEP)], dst_ref=pair_in.at[pl.ds(r, STEP)],
            send_sem=pair_s.at[q], recv_sem=pair_r.at[q],
            device_id={"tm": partner}, device_id_type=MESH,
        )

    def a_copy(d):
        to = peer(d)
        return pltpu.make_async_remote_copy(
            src_ref=coef.at[5, pl.ds(pl.multiple_of(to * BAND, BAND), BAND)],
            dst_ref=achip.at[chip],
            send_sem=a_s.at[d], recv_sem=a_r.at[d],
            device_id={"tm": to * 2 + core}, device_id_type=MESH,
        )

    def up_copy(q, d):
        to = peer(d)
        r = first_row(core, q)
        return pltpu.make_async_remote_copy(
            src_ref=merged.at[pl.ds(r, STEP), pl.ds(pl.multiple_of(to * BAND, BAND), BAND)],
            dst_ref=up_in.at[chip, pl.ds(r, STEP)],
            send_sem=up_s.at[q, d], recv_sem=up_r.at[q, d],
            device_id={"tm": to * 2 + core}, device_id_type=MESH,
        )

    def up_local(q):
        r = first_row(core, q)
        return pltpu.make_async_copy(
            merged.at[pl.ds(r, STEP), pl.ds(pl.multiple_of(chip * BAND, BAND), BAND)],
            up_in.at[chip, pl.ds(r, STEP)],
            up_s.at[q, 0],
        )

    def down_copy(q, d):
        to = peer(d)
        r = first_row(core, q)
        return pltpu.make_async_remote_copy(
            src_ref=down_out.at[to, pl.ds(r, STEP)],
            dst_ref=entry.at[pl.ds(r, STEP), pl.ds(pl.multiple_of(chip * BAND, BAND), BAND)],
            send_sem=down_s.at[q, d], recv_sem=down_r.at[q, d],
            device_id={"tm": to * 2 + core}, device_id_type=MESH,
        )

    def down_local(q):
        r = first_row(core, q)
        return pltpu.make_async_copy(
            down_out.at[chip, pl.ds(r, STEP)],
            entry.at[pl.ds(r, STEP), pl.ds(pl.multiple_of(chip * BAND, BAND), BAND)],
            down_s.at[q, 0],
        )

    def last_copy(q):
        r = first_row(core, q)
        return pltpu.make_async_remote_copy(
            src_ref=last_out.at[pl.ds(r, STEP)], dst_ref=last_in.at[pl.ds(r, STEP)],
            send_sem=last_s.at[q], recv_sem=last_r.at[q],
            device_id={"tm": partner}, device_id_type=MESH,
        )

    def last_arrival(q):
        r = first_row(1 - core, q)
        return pltpu.make_async_remote_copy(
            src_ref=last_out.at[pl.ds(r, STEP)], dst_ref=last_in.at[pl.ds(r, STEP)],
            send_sem=last_s.at[q], recv_sem=last_r.at[q],
            device_id={"tm": partner}, device_id_type=MESH,
        )

    def each(n0, n1, body):
        def run(i, carry):
            body(i)
            return carry

        lax.fori_loop(n0, n1, run, 0)

    other = 1 - core
    second = core.astype(F32)

    def conv_tile(q, t):
        r = first_row(other, q) + 2 * t
        theirs = convolved(r + HALF * other)
        h = first_row(core, q) + 2 * t + HALF * core
        ours = convolved(h)
        for e in range(2):
            value = driven(theirs, e)
            drive[r + HALF * other + e] = value
            pair_out[r + e] = value.astype(BF16)
        for e in range(2):
            drive[h + e] = driven(ours, e)

    a_local = pltpu.make_async_copy(
        coef.at[5, pl.ds(pl.multiple_of(chip * BAND, BAND), BAND)], achip.at[chip], a_s.at[0]
    )

    def coefficients():
        dec_copy.wait()
        mine = decs[0]
        theirs = column(lines[2])
        coef[1] = (1.0 - second) * theirs + second
        coef[2] = (1.0 - second) + second * mine
        coef[5] = mine * theirs
        coef[3] = (1.0 - second) * mine + second * (mine * theirs)
        each(1, CHIPS, lambda d: a_copy(d).start())
        a_local.start()

    def merge_half(q):
        pair_arrival(q).wait_recv()
        r0 = first_row(core, q)

        def merge(e):
            r = r0 + e
            own = drive[r + HALF * core]
            total = coef[1] * own + coef[2] * pair_in[r].astype(F32)
            merged[r] = total.astype(BF16)
            drive[r + HALF * core] = (1.0 - second) * own + second * total

        each(0, STEP, merge)
        each(1, CHIPS, lambda d: up_copy(q, d).start())
        up_local(q).start()

    def scan(q):
        each(1, CHIPS, lambda d: up_copy(q, d).wait_recv())
        up_local(q).wait()
        rows = pl.ds(first_row(core, q), STEP)
        state = jnp.zeros((STEP, BAND, WIDTH), F32)
        for i in range(CHIPS):
            down_out[i, rows] = state.astype(BF16)
            if i < CHIPS - 1:
                state = achip[i][None] * state + up_in[i, rows].astype(F32)
        each(1, CHIPS, lambda d: down_copy(q, d).start())
        down_local(q).start()

    reorder(1)
    reorder(2)
    for load in loads:
        load.wait()
    each(0, STEP // 2, lambda t: conv_tile(0, t))
    reorder(0)
    reorder(3)
    wo_load.wait()
    pl.semaphore_wait(barrier, CHIPS + 2)
    dec_copy.start()
    pair_copy(0).start()
    halo(0).start()
    halo(1).start()

    def front(q):
        @pl.when(q == CHUNKS - 1)
        def _():
            halo(0).wait()
            halo(1).wait()

            @pl.when(sp == 0)
            def _():
                xp[0] = jnp.zeros((CH, WIDTH), BF16)

            @pl.when(sp == 3)
            def _():
                xp[ROWS + 1] = jnp.zeros((CH, WIDTH), BF16)

        def step(t):
            conv_tile(q, t)

            @pl.when((q == 1) & (t == 0))
            def _():
                coefficients()
                merge_half(0)

        each(0, STEP // 2, step)
        pair_copy(q).start()

        @pl.when(q > 1)
        def _():
            merge_half(q - 1)

    each(1, CHUNKS, front)
    each(1, CHIPS, lambda d: a_copy(d).wait())
    a_local.wait()
    each(0, EARLY, scan)
    merge_half(CHUNKS - 1)
    each(EARLY, CHUNKS, scan)

    def project(h, memory):
        out = jnp.dot(
            wo[...], jnp.concatenate(memory, axis=1), preferred_element_type=F32
        )
        for e in range(2):
            row = h + e
            y_rows[row // GROUP, pl.ds(lax.rem(row, GROUP), CH, stride=GROUP), :] = (
                out[:, e * WIDTH : (e + 1) * WIDTH] + coef[4] * xp[row + 1].astype(F32)
            )

    def put(s, q):
        @pl.when(lax.rem(q, GROUP // STEP) == GROUP // STEP - 1)
        def _():
            b = (first_row(s, q) + HALF * s) // GROUP
            y_out[:, pl.ds(pl.multiple_of(b * GROUP, GROUP), GROUP)] = (
                y_rows[b].reshape(CH, GROUP, WIDTH).astype(BF16)
            )

    def finish(q):
        pair_copy(q).wait_send()
        each(1, CHIPS, lambda d: up_copy(q, d).wait_send())
        each(1, CHIPS, lambda d: down_copy(q, d).wait_recv())
        down_local(q).wait()
        r0 = first_row(core, q)

        def answer(e):
            r = r0 + e
            enter = entry[r].astype(F32)
            memory = coef[3] * enter + drive[r + HALF * core]
            drive[r + HALF * core] = memory
            last_out[r] = ((1.0 - second) * memory + second * enter).astype(BF16)

        each(0, STEP, answer)
        last_copy(q).start()

        def own_tile(t):
            h = r0 + 2 * t + HALF * core
            project(h, [drive[h + e].astype(BF16) for e in range(2)])

        each(0, STEP // 2, own_tile)
        put(core, q)
        last_arrival(q).wait_recv()
        r1 = first_row(other, q)

        def other_tile(t):
            r = r1 + 2 * t
            h = r + HALF * other
            project(
                h,
                [
                    (decs[0] * last_in[r + e].astype(F32) + drive[h + e]).astype(BF16)
                    for e in range(2)
                ],
            )

        each(0, STEP // 2, other_tile)
        put(other, q)
        last_copy(q).wait_send()
        each(1, CHIPS, lambda d: down_copy(q, d).wait_send())

    each(0, CHUNKS, finish)


def on_device(frames_in, conv_weight, out_weight, skip_gain, decays):
    rows = frames_in[0]
    pin = lambda a: pltpu.with_memory_space_constraint(a, pltpu.HBM)
    dma = pltpu.SemaphoreType.DMA
    y = pl.pallas_call(
        kernel,
        out_shape=jax.ShapeDtypeStruct((CH, ROWS, WIDTH), BF16),
        in_specs=[pl.BlockSpec(memory_space=pl.ANY)] * 5,
        out_specs=pl.BlockSpec(memory_space=pltpu.VMEM),
        scratch_shapes=[
            pltpu.VMEM((ROWS + 2, CH, WIDTH), BF16),
            pltpu.VMEM((3 * CH, 3 * CH), BF16),
            pltpu.VMEM((CH, CH), BF16),
            pltpu.VMEM((ROWS, CH, WIDTH), F32),
            pltpu.VMEM((6, CH, WIDTH), F32),
            pltpu.VMEM((1, CH, WIDTH), F32),
            pltpu.VMEM((CHIPS, BAND, WIDTH), F32),
            pltpu.VMEM((HALF, CH, WIDTH), BF16),
            pltpu.VMEM((HALF, CH, WIDTH), BF16),
            pltpu.VMEM((HALF, CH, WIDTH), BF16),
            pltpu.VMEM((CHIPS, HALF, BAND, WIDTH), BF16),
            pltpu.VMEM((CHIPS, HALF, BAND, WIDTH), BF16),
            pltpu.VMEM((HALF, CH, WIDTH), BF16),
            pltpu.VMEM((HALF, CH, WIDTH), BF16),
            pltpu.VMEM((HALF, CH, WIDTH), BF16),
            pltpu.VMEM((ROWS // GROUP, CH * GROUP, WIDTH), F32),
            pltpu.VMEM((ROWS // GROUP, CH, GROUP, WIDTH), BF16),
            pltpu.VMEM((CH * GROUP, WIDTH), F32),
            pltpu.VMEM((3, 1, CH), F32),
            dma((16,)),
            dma((2,)),
            dma((2,)),
            dma,
            dma,
            dma((CHIPS,)),
            dma((CHIPS,)),
            dma((CHUNKS,)),
            dma((CHUNKS,)),
            dma((CHUNKS, CHIPS)),
            dma((CHUNKS, CHIPS)),
            dma((CHUNKS, CHIPS)),
            dma((CHUNKS, CHIPS)),
            dma((CHUNKS,)),
            dma((CHUNKS,)),
        ],
        compiler_params=pltpu.CompilerParams(
            collective_id=0, has_side_effects=True, vmem_limit_bytes=VMEM_BYTES
        ),
    )(pin(rows), pin(conv_weight), pin(out_weight), pin(skip_gain[None, :]), pin(decays))
    return y[None]


def solution(mesh):
    placed = (P("tm", None, "space", None), P(), P(), P(), P("tm", None))
    return jax.shard_map(
        on_device,
        mesh=mesh,
        in_specs=placed,
        out_specs=P("tm", None, "space", None),
        check_vma=False,
    )
```

```python
import functools

import jax
import jax.numpy as jnp
from jax import lax
from jax.experimental import pallas as pl
from jax.experimental.pallas import tpu as pltpu
from jax.sharding import PartitionSpec as P

MESH = pl.DeviceIdType.MESH
ROWS = 32
HALF = 16
CH = 256
WIDTH = 128
CHIPS = 16
BAND = CH // CHIPS
CHUNKS = 4
GROUP = 8
EARLY = 0
VMEM_BYTES = 48 << 20
STEP = HALF // CHUNKS
F32 = jnp.float32
BF16 = jnp.bfloat16


def column(row):
    return jnp.transpose(jnp.broadcast_to(row, (WIDTH, CH)), (1, 0))


def kernel(
    x_hbm, w_hbm, wo_hbm, skip_hbm, dec_hbm, y_out,
    xp, wc, wo, drive, coef, decs, achip, pair_out, pair_in, merged, up_in, down_out, entry,
    last_out, last_in, y_rows, raw, stage, lines,
    load_sem, halo_s, halo_r, dec_s, dec_r, a_s, a_r, pair_s, pair_r, up_s, up_r,
    down_s, down_r, last_s, last_r, near_a, near_up, near_down,
):
    tm = lax.axis_index("tm")
    sp = lax.axis_index("space")
    chip = tm // 2
    core = lax.rem(tm, 2)
    partner = chip * 2 + (1 - core)
    above = lax.rem(sp + 3, 4)
    below = lax.rem(sp + 1, 4)

    def peer(d):
        return lax.rem(chip + d, CHIPS)

    barrier = pltpu.get_barrier_semaphore()

    def greet(d, carry):
        pl.semaphore_signal(
            barrier, inc=1, device_id={"tm": peer(d) * 2 + core}, device_id_type=MESH
        )
        return carry

    pl.semaphore_signal(barrier, inc=1, device_id={"tm": partner}, device_id_type=MESH)
    pl.semaphore_signal(barrier, inc=1, device_id={"space": above}, device_id_type=MESH)
    pl.semaphore_signal(barrier, inc=1, device_id={"space": below}, device_id_type=MESH)
    lax.fori_loop(1, CHIPS, greet, 0)

    x_loads = [
        pltpu.make_async_copy(
            x_hbm.at[:, pl.ds(GROUP * b, GROUP)], raw.at[b], load_sem.at[b]
        )
        for b in range(ROWS // GROUP)
    ]
    small_loads = [
        pltpu.make_async_copy(dec_hbm, lines.at[0], load_sem.at[6]),
        pltpu.make_async_copy(skip_hbm, lines.at[1], load_sem.at[7]),
    ]
    for load in small_loads:
        load.start()
    x_loads[1].start()
    x_loads[2].start()
    loads = []
    for i in range(3):
        for j in range(3):
            loads.append(
                pltpu.make_async_copy(
                    w_hbm.at[i, j],
                    wc.at[pl.ds(j * CH, CH), pl.ds(i * CH, CH)],
                    load_sem.at[5],
                )
            )
    wo_load = pltpu.make_async_copy(wo_hbm, wo, load_sem.at[4])
    for load in loads:
        load.start()
    x_loads[0].start()
    x_loads[3].start()
    wo_load.start()

    for load in small_loads:
        load.wait()
    own_decay = column(lines[0])
    decs[0] = own_decay
    coef[0] = jnp.sqrt(1.0 - own_decay * own_decay)
    coef[4] = column(lines[1])

    def halo(side):
        row, slot, target = ((ROWS, 0, below), (1, ROWS + 1, above))[side]
        return pltpu.make_async_remote_copy(
            src_ref=xp.at[row], dst_ref=xp.at[slot], send_sem=halo_s.at[side],
            recv_sem=halo_r.at[side], device_id={"space": target}, device_id_type=MESH,
        )

    def reorder(b):
        x_loads[b].wait()
        stage[...] = raw[b].astype(F32).reshape(CH * GROUP, WIDTH)

        def row(r):
            xp[1 + GROUP * b + r] = stage[pl.ds(r, CH, stride=GROUP), :].astype(BF16)

        for r in range(GROUP):
            row(r)

    dec_copy = pltpu.make_async_remote_copy(
        src_ref=lines.at[0], dst_ref=lines.at[2], send_sem=dec_s, recv_sem=dec_r,
        device_id={"tm": partner}, device_id_type=MESH,
    )

    def first_row(s, q):
        return (1 - s) * (HALF - STEP * (q + 1)) + s * (STEP * q)

    lane = lax.broadcasted_iota(jnp.int32, (CH, WIDTH), 1)

    def convolved(h):
        view = [xp[h + i] for i in range(4)]
        right = jnp.concatenate(
            [jnp.concatenate([view[i], view[i + 1]], axis=1) for i in range(3)], axis=0
        )
        return jnp.dot(wc[...], right, preferred_element_type=F32)

    def driven(acc, e):
        part = acc[:, e * WIDTH : (e + 1) * WIDTH]
        left = jnp.where(lane == 0, 0.0, pltpu.roll(part[0:CH], 1, 1))
        after = jnp.where(lane == WIDTH - 1, 0.0, pltpu.roll(part[2 * CH :], WIDTH - 1, 1))
        return coef[0] * (left + part[CH : 2 * CH] + after)

    def pair_copy(q):
        r = first_row(1 - core, q)
        return pltpu.make_async_remote_copy(
            src_ref=pair_out.at[pl.ds(r, STEP)], dst_ref=pair_in.at[pl.ds(r, STEP)],
            send_sem=pair_s.at[q], recv_sem=pair_r.at[q],
            device_id={"tm": partner}, device_id_type=MESH,
        )

    def pair_arrival(q):
        r = first_row(core, q)
        return pltpu.make_async_remote_copy(
            src_ref=pair_out.at[pl.ds(r, STEP)], dst_ref=pair_in.at[pl.ds(r, STEP)],
            send_sem=pair_s.at[q], recv_sem=pair_r.at[q],
            device_id={"tm": partner}, device_id_type=MESH,
        )

    def a_copy(d):
        to = peer(d)
        return pltpu.make_async_remote_copy(
            src_ref=coef.at[5, pl.ds(pl.multiple_of(to * BAND, BAND), BAND)],
            dst_ref=achip.at[chip],
            send_sem=a_s, recv_sem=a_r,
            device_id={"tm": to * 2 + core}, device_id_type=MESH,
        )

    def up_copy(q, d):
        to = peer(d)
        r = first_row(core, q)
        return pltpu.make_async_remote_copy(
            src_ref=merged.at[pl.ds(r, STEP), pl.ds(pl.multiple_of(to * BAND, BAND), BAND)],
            dst_ref=up_in.at[chip, pl.ds(r, STEP)],
            send_sem=up_s.at[q], recv_sem=up_r.at[q],
            device_id={"tm": to * 2 + core}, device_id_type=MESH,
        )

    def up_local(q):
        r = first_row(core, q)
        return pltpu.make_async_copy(
            merged.at[pl.ds(r, STEP), pl.ds(pl.multiple_of(chip * BAND, BAND), BAND)],
            up_in.at[chip, pl.ds(r, STEP)],
            near_up.at[q],
        )

    def down_copy(q, d):
        to = peer(d)
        r = first_row(core, q)
        return pltpu.make_async_remote_copy(
            src_ref=down_out.at[to, pl.ds(r, STEP)],
            dst_ref=entry.at[pl.ds(r, STEP), pl.ds(pl.multiple_of(chip * BAND, BAND), BAND)],
            send_sem=down_s.at[q], recv_sem=down_r.at[q],
            device_id={"tm": to * 2 + core}, device_id_type=MESH,
        )

    def down_local(q):
        r = first_row(core, q)
        return pltpu.make_async_copy(
            down_out.at[chip, pl.ds(r, STEP)],
            entry.at[pl.ds(r, STEP), pl.ds(pl.multiple_of(chip * BAND, BAND), BAND)],
            near_down.at[q],
        )

    def last_copy(q):
        r = first_row(core, q)
        return pltpu.make_async_remote_copy(
            src_ref=last_out.at[pl.ds(r, STEP)], dst_ref=last_in.at[pl.ds(r, STEP)],
            send_sem=last_s.at[q], recv_sem=last_r.at[q],
            device_id={"tm": partner}, device_id_type=MESH,
        )

    def last_arrival(q):
        r = first_row(1 - core, q)
        return pltpu.make_async_remote_copy(
            src_ref=last_out.at[pl.ds(r, STEP)], dst_ref=last_in.at[pl.ds(r, STEP)],
            send_sem=last_s.at[q], recv_sem=last_r.at[q],
            device_id={"tm": partner}, device_id_type=MESH,
        )

    def a_all():
        part = achip.at[pl.ds(0, CHIPS - 1)]
        return pltpu.make_async_remote_copy(
            src_ref=part, dst_ref=part, send_sem=a_s, recv_sem=a_r,
            device_id={"tm": partner}, device_id_type=MESH,
        )

    def up_all(q):
        part = up_in.at[pl.ds(0, CHIPS - 1), pl.ds(first_row(core, q), STEP)]
        return pltpu.make_async_remote_copy(
            src_ref=part, dst_ref=part, send_sem=up_s.at[q], recv_sem=up_r.at[q],
            device_id={"tm": partner}, device_id_type=MESH,
        )

    def down_all(q):
        part = down_out.at[pl.ds(0, CHIPS - 1), pl.ds(first_row(core, q), STEP)]
        return pltpu.make_async_remote_copy(
            src_ref=part, dst_ref=part, send_sem=down_s.at[q], recv_sem=down_r.at[q],
            device_id={"tm": partner}, device_id_type=MESH,
        )

    def each(n0, n1, body):
        def run(i, carry):
            body(i)
            return carry

        lax.fori_loop(n0, n1, run, 0)

    other = 1 - core
    second = core.astype(F32)

    def conv_tile(q, t):
        r = first_row(other, q) + 2 * t
        theirs = convolved(r + HALF * other)
        h = first_row(core, q) + 2 * t + HALF * core
        ours = convolved(h)
        for e in range(2):
            value = driven(theirs, e)
            drive[r + HALF * other + e] = value
            pair_out[r + e] = value.astype(BF16)
        for e in range(2):
            drive[h + e] = driven(ours, e)

    a_local = pltpu.make_async_copy(
        coef.at[5, pl.ds(pl.multiple_of(chip * BAND, BAND), BAND)], achip.at[chip], near_a
    )

    def coefficients():
        dec_copy.wait()
        mine = decs[0]
        theirs = column(lines[2])
        coef[1] = (1.0 - second) * theirs + second
        coef[2] = (1.0 - second) + second * mine
        coef[5] = mine * theirs
        coef[3] = (1.0 - second) * mine + second * (mine * theirs)

    def merge_half(q):
        pair_arrival(q).wait_recv()
        r0 = first_row(core, q)

        def merge(e):
            r = r0 + e
            own = drive[r + HALF * core]
            total = coef[1] * own + coef[2] * pair_in[r].astype(F32)
            merged[r] = total.astype(BF16)
            drive[r + HALF * core] = (1.0 - second) * own + second * total

        each(0, STEP, merge)
        each(1, CHIPS, lambda d: up_copy(q, d).start())
        up_local(q).start()

    def scan(q):
        up_all(q).wait_recv()
        up_local(q).wait()
        rows = pl.ds(first_row(core, q), STEP)
        state = jnp.zeros((STEP, BAND, WIDTH), F32)
        for i in range(CHIPS):
            down_out[i, rows] = state.astype(BF16)
            if i < CHIPS - 1:
                state = achip[i][None] * state + up_in[i, rows].astype(F32)
        each(1, CHIPS, lambda d: down_copy(q, d).start())
        down_local(q).start()

    reorder(1)
    reorder(2)
    pltpu.make_async_copy(wc, wc, load_sem.at[5]).wait()
    each(0, STEP // 2, lambda t: conv_tile(0, t))
    reorder(0)
    reorder(3)
    wo_load.wait()
    pl.semaphore_wait(barrier, CHIPS + 2)
    dec_copy.start()
    pair_copy(0).start()
    halo(0).start()
    halo(1).start()

    def front(q):
        @pl.when(q == CHUNKS - 1)
        def _():
            halo(0).wait()
            halo(1).wait()

            @pl.when(sp == 0)
            def _():
                xp[0] = jnp.zeros((CH, WIDTH), BF16)

            @pl.when(sp == 3)
            def _():
                xp[ROWS + 1] = jnp.zeros((CH, WIDTH), BF16)

        def step(t):
            conv_tile(q, t)

            @pl.when((q == 1) & (t == 0))
            def _():
                coefficients()
                merge_half(0)
                each(1, CHIPS, lambda d: a_copy(d).start())
                a_local.start()

        each(0, STEP // 2, step)
        pair_copy(q).start()

        @pl.when(q > 1)
        def _():
            merge_half(q - 1)

    each(1, CHUNKS, front)
    a_all().wait()
    a_local.wait()
    each(0, EARLY, scan)
    merge_half(CHUNKS - 1)
    each(EARLY, CHUNKS, scan)

    def project(h, memory):
        out = jnp.dot(
            wo[...], jnp.concatenate(memory, axis=1), preferred_element_type=F32
        )
        for e in range(2):
            row = h + e
            y_rows[row // GROUP, pl.ds(lax.rem(row, GROUP), CH, stride=GROUP), :] = (
                out[:, e * WIDTH : (e + 1) * WIDTH] + coef[4] * xp[row + 1].astype(F32)
            )

    def put(s, q):
        @pl.when(lax.rem(q, GROUP // STEP) == GROUP // STEP - 1)
        def _():
            b = (first_row(s, q) + HALF * s) // GROUP
            y_out[:, pl.ds(pl.multiple_of(b * GROUP, GROUP), GROUP)] = (
                y_rows[b].reshape(CH, GROUP, WIDTH).astype(BF16)
            )

    def finish(q):
        pair_copy(q).wait_send()
        up_all(q).wait_send()
        down_all(q).wait_recv()
        down_local(q).wait()
        r0 = first_row(core, q)

        def answer(e):
            r = r0 + e
            enter = entry[r].astype(F32)
            memory = coef[3] * enter + drive[r + HALF * core]
            drive[r + HALF * core] = memory
            last_out[r] = ((1.0 - second) * memory + second * enter).astype(BF16)

        each(0, STEP, answer)
        last_copy(q).start()

        def own_tile(t):
            h = r0 + 2 * t + HALF * core
            project(h, [drive[h + e].astype(BF16) for e in range(2)])

        each(0, STEP // 2, own_tile)
        put(core, q)
        last_arrival(q).wait_recv()
        r1 = first_row(other, q)

        def other_tile(t):
            r = r1 + 2 * t
            h = r + HALF * other
            project(
                h,
                [
                    (decs[0] * last_in[r + e].astype(F32) + drive[h + e]).astype(BF16)
                    for e in range(2)
                ],
            )

        each(0, STEP // 2, other_tile)
        put(other, q)
        last_copy(q).wait_send()
        down_all(q).wait_send()

    each(0, CHUNKS, finish)


def on_device(frames_in, conv_weight, out_weight, skip_gain, decays):
    rows = frames_in[0]
    pin = lambda a: pltpu.with_memory_space_constraint(a, pltpu.HBM)
    dma = pltpu.SemaphoreType.DMA
    y = pl.pallas_call(
        kernel,
        out_shape=jax.ShapeDtypeStruct((CH, ROWS, WIDTH), BF16),
        in_specs=[pl.BlockSpec(memory_space=pl.ANY)] * 5,
        out_specs=pl.BlockSpec(memory_space=pltpu.VMEM),
        scratch_shapes=[
            pltpu.VMEM((ROWS + 2, CH, WIDTH), BF16),
            pltpu.VMEM((3 * CH, 3 * CH), BF16),
            pltpu.VMEM((CH, CH), BF16),
            pltpu.VMEM((ROWS, CH, WIDTH), F32),
            pltpu.VMEM((6, CH, WIDTH), F32),
            pltpu.VMEM((1, CH, WIDTH), F32),
            pltpu.VMEM((CHIPS, BAND, WIDTH), F32),
            pltpu.VMEM((HALF, CH, WIDTH), BF16),
            pltpu.VMEM((HALF, CH, WIDTH), BF16),
            pltpu.VMEM((HALF, CH, WIDTH), BF16),
            pltpu.VMEM((CHIPS, HALF, BAND, WIDTH), BF16),
            pltpu.VMEM((CHIPS, HALF, BAND, WIDTH), BF16),
            pltpu.VMEM((HALF, CH, WIDTH), BF16),
            pltpu.VMEM((HALF, CH, WIDTH), BF16),
            pltpu.VMEM((HALF, CH, WIDTH), BF16),
            pltpu.VMEM((ROWS // GROUP, CH * GROUP, WIDTH), F32),
            pltpu.VMEM((ROWS // GROUP, CH, GROUP, WIDTH), BF16),
            pltpu.VMEM((CH * GROUP, WIDTH), F32),
            pltpu.VMEM((3, 1, CH), F32),
            dma((8,)),
            dma((2,)),
            dma((2,)),
            dma,
            dma,
            dma,
            dma,
            dma((CHUNKS,)),
            dma((CHUNKS,)),
            dma((CHUNKS,)),
            dma((CHUNKS,)),
            dma((CHUNKS,)),
            dma((CHUNKS,)),
            dma((CHUNKS,)),
            dma((CHUNKS,)),
            dma,
            dma((CHUNKS,)),
            dma((CHUNKS,)),
        ],
        compiler_params=pltpu.CompilerParams(
            collective_id=0, has_side_effects=True, vmem_limit_bytes=VMEM_BYTES
        ),
    )(pin(rows), pin(conv_weight), pin(out_weight), pin(skip_gain[None, :]), pin(decays))
    return y[None]


def solution(mesh):
    placed = (P("tm", None, "space", None), P(), P(), P(), P("tm", None))
    return jax.shard_map(
        on_device,
        mesh=mesh,
        in_specs=placed,
        out_specs=P("tm", None, "space", None),
        check_vma=False,
    )
```

```python
import functools

import jax
import jax.numpy as jnp
from jax import lax
from jax.experimental import pallas as pl
from jax.experimental.pallas import tpu as pltpu
from jax.sharding import PartitionSpec as P

MESH = pl.DeviceIdType.MESH
ROWS = 32
HALF = 16
CH = 256
WIDTH = 128
CHIPS = 16
BAND = CH // CHIPS
CHUNKS = 8
GROUP = 8
EARLY = 0
VMEM_BYTES = 48 << 20
STEP = HALF // CHUNKS
RETURNS = 8
BACK = HALF // RETURNS
F32 = jnp.float32
BF16 = jnp.bfloat16


def column(row):
    return jnp.transpose(jnp.broadcast_to(row, (WIDTH, CH)), (1, 0))


def kernel(
    x_hbm, w_hbm, wo_hbm, skip_hbm, dec_hbm, y_out,
    xp, wc, wo, drive, coef, decs, achip, pair_out, pair_in, merged, up_in, down_out, entry,
    last_out, last_in, y_rows, raw, stage, lines,
    load_sem, halo_s, halo_r, dec_s, dec_r, a_s, a_r, pair_s, pair_r, up_s, up_r,
    down_s, down_r, last_s, last_r,
):
    tm = lax.axis_index("tm")
    sp = lax.axis_index("space")
    chip = tm // 2
    core = lax.rem(tm, 2)
    partner = chip * 2 + (1 - core)
    above = lax.rem(sp + 3, 4)
    below = lax.rem(sp + 1, 4)

    def peer(d):
        return lax.rem(chip + d, CHIPS)

    barrier = pltpu.get_barrier_semaphore()

    def greet(d, carry):
        pl.semaphore_signal(
            barrier, inc=1, device_id={"tm": peer(d) * 2 + core}, device_id_type=MESH
        )
        return carry

    pl.semaphore_signal(barrier, inc=1, device_id={"tm": partner}, device_id_type=MESH)
    pl.semaphore_signal(barrier, inc=1, device_id={"space": above}, device_id_type=MESH)
    pl.semaphore_signal(barrier, inc=1, device_id={"space": below}, device_id_type=MESH)
    lax.fori_loop(1, CHIPS, greet, 0)

    x_loads = [
        pltpu.make_async_copy(
            x_hbm.at[:, pl.ds(GROUP * b, GROUP)], raw.at[b], load_sem.at[b]
        )
        for b in range(ROWS // GROUP)
    ]
    small_loads = [
        pltpu.make_async_copy(dec_hbm, lines.at[0], load_sem.at[6]),
        pltpu.make_async_copy(skip_hbm, lines.at[1], load_sem.at[7]),
    ]
    for load in small_loads:
        load.start()
    x_loads[1].start()
    x_loads[2].start()
    loads = []
    for i in range(3):
        for j in range(3):
            loads.append(
                pltpu.make_async_copy(
                    w_hbm.at[i, j],
                    wc.at[pl.ds(j * CH, CH), pl.ds(i * CH, CH)],
                    load_sem.at[5],
                )
            )
    wo_load = pltpu.make_async_copy(wo_hbm, wo, load_sem.at[4])
    for load in loads:
        load.start()
    x_loads[0].start()
    x_loads[3].start()
    wo_load.start()

    for load in small_loads:
        load.wait()
    own_decay = column(lines[0])
    decs[0] = own_decay
    coef[0] = jnp.sqrt(1.0 - own_decay * own_decay)
    coef[4] = column(lines[1])

    def halo(side):
        row, slot, target = ((ROWS, 0, below), (1, ROWS + 1, above))[side]
        return pltpu.make_async_remote_copy(
            src_ref=xp.at[row], dst_ref=xp.at[slot], send_sem=halo_s.at[side],
            recv_sem=halo_r.at[side], device_id={"space": target}, device_id_type=MESH,
        )

    def reorder(b):
        x_loads[b].wait()
        stage[...] = raw[b].astype(F32).reshape(CH * GROUP, WIDTH)

        def row(r):
            xp[1 + GROUP * b + r] = stage[pl.ds(r, CH, stride=GROUP), :].astype(BF16)

        for r in range(GROUP):
            row(r)

    dec_copy = pltpu.make_async_remote_copy(
        src_ref=lines.at[0], dst_ref=lines.at[2], send_sem=dec_s, recv_sem=dec_r,
        device_id={"tm": partner}, device_id_type=MESH,
    )

    def first_row(s, q):
        return (1 - s) * (HALF - STEP * (q + 1)) + s * (STEP * q)

    def back_row(s, q):
        return (1 - s) * (HALF - BACK * (q + 1)) + s * (BACK * q)

    lane = lax.broadcasted_iota(jnp.int32, (CH, WIDTH), 1)

    def convolved(h):
        view = [xp[h + i] for i in range(4)]
        right = jnp.concatenate(
            [jnp.concatenate([view[i], view[i + 1]], axis=1) for i in range(3)], axis=0
        )
        return jnp.dot(wc[...], right, preferred_element_type=F32)

    def driven(acc, e):
        part = acc[:, e * WIDTH : (e + 1) * WIDTH]
        left = jnp.where(lane == 0, 0.0, pltpu.roll(part[0:CH], 1, 1))
        after = jnp.where(lane == WIDTH - 1, 0.0, pltpu.roll(part[2 * CH :], WIDTH - 1, 1))
        return coef[0] * (left + part[CH : 2 * CH] + after)

    def pair_copy(q):
        r = first_row(1 - core, q)
        return pltpu.make_async_remote_copy(
            src_ref=pair_out.at[pl.ds(r, STEP)], dst_ref=pair_in.at[pl.ds(r, STEP)],
            send_sem=pair_s, recv_sem=pair_r.at[q],
            device_id={"tm": partner}, device_id_type=MESH,
        )

    def pair_arrival(q):
        r = first_row(core, q)
        return pltpu.make_async_remote_copy(
            src_ref=pair_out.at[pl.ds(r, STEP)], dst_ref=pair_in.at[pl.ds(r, STEP)],
            send_sem=pair_s, recv_sem=pair_r.at[q],
            device_id={"tm": partner}, device_id_type=MESH,
        )

    def a_copy(d):
        to = peer(d)
        return pltpu.make_async_remote_copy(
            src_ref=coef.at[5, pl.ds(pl.multiple_of(to * BAND, BAND), BAND)],
            dst_ref=achip.at[chip],
            send_sem=a_s, recv_sem=a_r,
            device_id={"tm": to * 2 + core}, device_id_type=MESH,
        )

    def up_copy(q, d):
        to = peer(d)
        r = first_row(core, q)
        return pltpu.make_async_remote_copy(
            src_ref=merged.at[pl.ds(r, STEP), pl.ds(pl.multiple_of(to * BAND, BAND), BAND)],
            dst_ref=up_in.at[chip, pl.ds(r, STEP)],
            send_sem=up_s, recv_sem=up_r.at[q],
            device_id={"tm": to * 2 + core}, device_id_type=MESH,
        )

    def up_local(q):
        r = first_row(core, q)
        return pltpu.make_async_copy(
            merged.at[pl.ds(r, STEP), pl.ds(pl.multiple_of(chip * BAND, BAND), BAND)],
            up_in.at[chip, pl.ds(r, STEP)],
            up_r.at[q],
        )

    def down_copy(q, d):
        to = peer(d)
        r = back_row(core, q)
        return pltpu.make_async_remote_copy(
            src_ref=down_out.at[to, pl.ds(r, BACK)],
            dst_ref=entry.at[pl.ds(r, BACK), pl.ds(pl.multiple_of(chip * BAND, BAND), BAND)],
            send_sem=down_s, recv_sem=down_r.at[q],
            device_id={"tm": to * 2 + core}, device_id_type=MESH,
        )

    def down_local(q):
        r = back_row(core, q)
        return pltpu.make_async_copy(
            down_out.at[chip, pl.ds(r, BACK)],
            entry.at[pl.ds(r, BACK), pl.ds(pl.multiple_of(chip * BAND, BAND), BAND)],
            down_r.at[q],
        )

    def last_copy(q):
        r = back_row(core, q)
        return pltpu.make_async_remote_copy(
            src_ref=last_out.at[pl.ds(r, BACK)], dst_ref=last_in.at[pl.ds(r, BACK)],
            send_sem=last_s, recv_sem=last_r.at[q],
            device_id={"tm": partner}, device_id_type=MESH,
        )

    def last_arrival(q):
        r = back_row(1 - core, q)
        return pltpu.make_async_remote_copy(
            src_ref=last_out.at[pl.ds(r, BACK)], dst_ref=last_in.at[pl.ds(r, BACK)],
            send_sem=last_s, recv_sem=last_r.at[q],
            device_id={"tm": partner}, device_id_type=MESH,
        )

    def arrived(part, sem):
        pltpu.make_async_copy(part, part, sem).wait()

    def sent(part, sem):
        pltpu.make_async_copy(part, part, sem).wait()

    def each(n0, n1, body):
        def run(i, carry):
            body(i)
            return carry

        lax.fori_loop(n0, n1, run, 0)

    other = 1 - core
    second = core.astype(F32)

    def conv_tile(q, t):
        r = first_row(other, q) + 2 * t
        theirs = convolved(r + HALF * other)
        h = first_row(core, q) + 2 * t + HALF * core
        ours = convolved(h)
        for e in range(2):
            value = driven(theirs, e)
            drive[r + HALF * other + e] = value
            pair_out[r + e] = value.astype(BF16)
        for e in range(2):
            drive[h + e] = driven(ours, e)

    a_local = pltpu.make_async_copy(
        coef.at[5, pl.ds(pl.multiple_of(chip * BAND, BAND), BAND)], achip.at[chip], a_r
    )

    def coefficients():
        dec_copy.wait()
        mine = decs[0]
        theirs = column(lines[2])
        coef[1] = (1.0 - second) * theirs + second
        coef[2] = (1.0 - second) + second * mine
        coef[5] = mine * theirs
        coef[3] = (1.0 - second) * mine + second * (mine * theirs)

    def merge_half(q):
        pair_arrival(q).wait_recv()
        r0 = first_row(core, q)

        def merge(e):
            r = r0 + e
            own = drive[r + HALF * core]
            total = coef[1] * own + coef[2] * pair_in[r].astype(F32)
            merged[r] = total.astype(BF16)
            drive[r + HALF * core] = (1.0 - second) * own + second * total

        each(0, STEP, merge)
        each(1, CHIPS, lambda d: up_copy(q, d).start())
        up_local(q).start()

    def scan(q):
        arrived(up_in.at[:, pl.ds(first_row(core, q), STEP)], up_r.at[q])
        rows = pl.ds(first_row(core, q), STEP)
        state = jnp.zeros((STEP, BAND, WIDTH), F32)
        for i in range(CHIPS):
            down_out[i, rows] = state.astype(BF16)
            if i < CHIPS - 1:
                state = achip[i][None] * state + up_in[i, rows].astype(F32)

        def give(p):
            each(1, CHIPS, lambda d: down_copy(p, d).start())
            down_local(p).start()

        each(STEP // BACK * q, STEP // BACK * (q + 1), give)

    reorder(1)
    reorder(2)
    pltpu.make_async_copy(wc, wc, load_sem.at[5]).wait()
    each(0, STEP // 2, lambda t: conv_tile(0, t))
    reorder(0)
    reorder(3)
    wo_load.wait()
    pl.semaphore_wait(barrier, CHIPS + 2)
    dec_copy.start()
    pair_copy(0).start()
    halo(0).start()
    halo(1).start()

    def front(q):
        @pl.when(q == CHUNKS - 1)
        def _():
            halo(0).wait()
            halo(1).wait()

            @pl.when(sp == 0)
            def _():
                xp[0] = jnp.zeros((CH, WIDTH), BF16)

            @pl.when(sp == 3)
            def _():
                xp[ROWS + 1] = jnp.zeros((CH, WIDTH), BF16)

        def step(t):
            conv_tile(q, t)

            @pl.when((q == 1) & (t == 0))
            def _():
                coefficients()
                merge_half(0)
                each(1, CHIPS, lambda d: a_copy(d).start())
                a_local.start()

        each(0, STEP // 2, step)
        pair_copy(q).start()

        @pl.when(q > 1)
        def _():
            merge_half(q - 1)

    each(1, CHUNKS, front)
    arrived(achip, a_r)
    each(0, EARLY, scan)
    merge_half(CHUNKS - 1)
    each(EARLY, CHUNKS, scan)

    def project(h, memory):
        out = jnp.dot(
            wo[...], jnp.concatenate(memory, axis=1), preferred_element_type=F32
        )
        for e in range(2):
            row = h + e
            y_rows[row // GROUP, pl.ds(lax.rem(row, GROUP), CH, stride=GROUP), :] = (
                out[:, e * WIDTH : (e + 1) * WIDTH] + coef[4] * xp[row + 1].astype(F32)
            )

    def put(s, q):
        @pl.when(lax.rem(q, GROUP // BACK) == GROUP // BACK - 1)
        def _():
            b = (back_row(s, q) + HALF * s) // GROUP
            y_out[:, pl.ds(pl.multiple_of(b * GROUP, GROUP), GROUP)] = (
                y_rows[b].reshape(CH, GROUP, WIDTH).astype(BF16)
            )

    def finish_own(q):
        arrived(entry.at[pl.ds(back_row(core, q), BACK)], down_r.at[q])
        r0 = back_row(core, q)

        def answer(e):
            r = r0 + e
            enter = entry[r].astype(F32)
            memory = coef[3] * enter + drive[r + HALF * core]
            drive[r + HALF * core] = memory
            last_out[r] = ((1.0 - second) * memory + second * enter).astype(BF16)

        each(0, BACK, answer)
        last_copy(q).start()

        def tile(t):
            h = r0 + 2 * t + HALF * core
            project(h, [drive[h + e].astype(BF16) for e in range(2)])

        each(0, BACK // 2, tile)
        put(core, q)

    def finish_other(q):
        last_arrival(q).wait_recv()
        r0 = back_row(other, q)

        def tile(t):
            r = r0 + 2 * t
            h = r + HALF * other
            project(
                h,
                [
                    (decs[0] * last_in[r + e].astype(F32) + drive[h + e]).astype(BF16)
                    for e in range(2)
                ],
            )

        each(0, BACK // 2, tile)
        put(other, q)

    def finish(q):
        @pl.when(q < RETURNS)
        def _():
            finish_own(q)

        @pl.when(q > 0)
        def _():
            finish_other(q - 1)

    each(0, RETURNS + 1, finish)
    sent(pair_out, pair_s)
    sent(last_out, last_s)
    sent(achip.at[pl.ds(0, CHIPS - 1)], a_s)
    sent(up_in.at[pl.ds(0, CHIPS - 1)], up_s)
    sent(down_out.at[pl.ds(0, CHIPS - 1)], down_s)


def on_device(frames_in, conv_weight, out_weight, skip_gain, decays):
    rows = frames_in[0]
    pin = lambda a: pltpu.with_memory_space_constraint(a, pltpu.HBM)
    dma = pltpu.SemaphoreType.DMA
    y = pl.pallas_call(
        kernel,
        out_shape=jax.ShapeDtypeStruct((CH, ROWS, WIDTH), BF16),
        in_specs=[pl.BlockSpec(memory_space=pl.ANY)] * 5,
        out_specs=pl.BlockSpec(memory_space=pltpu.VMEM),
        scratch_shapes=[
            pltpu.VMEM((ROWS + 2, CH, WIDTH), BF16),
            pltpu.VMEM((3 * CH, 3 * CH), BF16),
            pltpu.VMEM((CH, CH), BF16),
            pltpu.VMEM((ROWS, CH, WIDTH), F32),
            pltpu.VMEM((6, CH, WIDTH), F32),
            pltpu.VMEM((1, CH, WIDTH), F32),
            pltpu.VMEM((CHIPS, BAND, WIDTH), F32),
            pltpu.VMEM((HALF, CH, WIDTH), BF16),
            pltpu.VMEM((HALF, CH, WIDTH), BF16),
            pltpu.VMEM((HALF, CH, WIDTH), BF16),
            pltpu.VMEM((CHIPS, HALF, BAND, WIDTH), BF16),
            pltpu.VMEM((CHIPS, HALF, BAND, WIDTH), BF16),
            pltpu.VMEM((HALF, CH, WIDTH), BF16),
            pltpu.VMEM((HALF, CH, WIDTH), BF16),
            pltpu.VMEM((HALF, CH, WIDTH), BF16),
            pltpu.VMEM((ROWS // GROUP, CH * GROUP, WIDTH), F32),
            pltpu.VMEM((ROWS // GROUP, CH, GROUP, WIDTH), BF16),
            pltpu.VMEM((CH * GROUP, WIDTH), F32),
            pltpu.VMEM((3, 1, CH), F32),
            dma((8,)),
            dma((2,)),
            dma((2,)),
            dma,
            dma,
            dma,
            dma,
            dma,
            dma((CHUNKS,)),
            dma,
            dma((CHUNKS,)),
            dma,
            dma((RETURNS,)),
            dma,
            dma((RETURNS,)),
        ],
        compiler_params=pltpu.CompilerParams(
            collective_id=0, has_side_effects=True, vmem_limit_bytes=VMEM_BYTES
        ),
    )(pin(rows), pin(conv_weight), pin(out_weight), pin(skip_gain[None, :]), pin(decays))
    return y[None]


def solution(mesh):
    placed = (P("tm", None, "space", None), P(), P(), P(), P("tm", None))
    return jax.shard_map(
        on_device,
        mesh=mesh,
        in_specs=placed,
        out_specs=P("tm", None, "space", None),
        check_vma=False,
    )
```

```python
import functools

import jax
import jax.numpy as jnp
from jax import lax
from jax.experimental import pallas as pl
from jax.experimental.pallas import tpu as pltpu
from jax.sharding import PartitionSpec as P

MESH = pl.DeviceIdType.MESH
ROWS = 32
HALF = 16
CH = 256
WIDTH = 128
CHIPS = 16
BAND = CH // CHIPS
CHUNKS = 8
GROUP = 8
EARLY = 0
VMEM_BYTES = 48 << 20
STEP = HALF // CHUNKS
RETURNS = 8
BACK = HALF // RETURNS
F32 = jnp.float32
BF16 = jnp.bfloat16


def column(row):
    return jnp.transpose(jnp.broadcast_to(row, (WIDTH, CH)), (1, 0))


def kernel(
    x_hbm, w_hbm, wo_hbm, skip_hbm, dec_hbm, y_out,
    xp, wc, wo, drive, coef, decs, achip, pair_out, pair_in, merged, up_in, down_out, entry,
    last_out, last_in, y_rows, raw, stage, lines,
    load_sem, halo_s, halo_r, dec_s, dec_r, a_s, a_r, pair_s, pair_r, up_s, up_r,
    down_s, down_r, last_s, last_r,
):
    tm = lax.axis_index("tm")
    sp = lax.axis_index("space")
    chip = tm // 2
    core = lax.rem(tm, 2)
    partner = chip * 2 + (1 - core)
    above = lax.rem(sp + 3, 4)
    below = lax.rem(sp + 1, 4)

    def peer(d):
        return lax.rem(chip + d, CHIPS)

    barrier = pltpu.get_barrier_semaphore()

    def greet(d, carry):
        pl.semaphore_signal(
            barrier, inc=1, device_id={"tm": peer(d) * 2 + core}, device_id_type=MESH
        )
        return carry

    pl.semaphore_signal(barrier, inc=1, device_id={"tm": partner}, device_id_type=MESH)
    pl.semaphore_signal(barrier, inc=1, device_id={"space": above}, device_id_type=MESH)
    pl.semaphore_signal(barrier, inc=1, device_id={"space": below}, device_id_type=MESH)
    lax.fori_loop(1, CHIPS, greet, 0)

    x_loads = [
        pltpu.make_async_copy(
            x_hbm.at[:, pl.ds(GROUP * b, GROUP)], raw.at[b], load_sem.at[b]
        )
        for b in range(ROWS // GROUP)
    ]
    small_loads = [
        pltpu.make_async_copy(dec_hbm, lines.at[0], load_sem.at[6]),
        pltpu.make_async_copy(skip_hbm, lines.at[1], load_sem.at[7]),
    ]
    for load in small_loads:
        load.start()
    x_loads[1].start()
    x_loads[2].start()
    loads = []
    for i in range(3):
        for j in range(3):
            loads.append(
                pltpu.make_async_copy(
                    w_hbm.at[i, j],
                    wc.at[pl.ds(j * CH, CH), pl.ds(i * CH, CH)],
                    load_sem.at[5],
                )
            )
    wo_load = pltpu.make_async_copy(wo_hbm, wo, load_sem.at[4])
    for load in loads:
        load.start()
    x_loads[0].start()
    x_loads[3].start()
    wo_load.start()

    for load in small_loads:
        load.wait()
    own_decay = column(lines[0])
    decs[0] = own_decay
    coef[0] = jnp.sqrt(1.0 - own_decay * own_decay)
    coef[4] = column(lines[1])

    def halo(side):
        row, slot, target = ((ROWS, 0, below), (1, ROWS + 1, above))[side]
        return pltpu.make_async_remote_copy(
            src_ref=xp.at[row], dst_ref=xp.at[slot], send_sem=halo_s.at[side],
            recv_sem=halo_r.at[side], device_id={"space": target}, device_id_type=MESH,
        )

    def reorder(b):
        x_loads[b].wait()
        stage[...] = raw[b].astype(F32).reshape(CH * GROUP, WIDTH)

        def row(r):
            xp[1 + GROUP * b + r] = stage[pl.ds(r, CH, stride=GROUP), :].astype(BF16)

        for r in range(GROUP):
            row(r)

    dec_copy = pltpu.make_async_remote_copy(
        src_ref=lines.at[0], dst_ref=lines.at[2], send_sem=dec_s, recv_sem=dec_r,
        device_id={"tm": partner}, device_id_type=MESH,
    )

    def first_row(s, q):
        return (1 - s) * (HALF - STEP * (q + 1)) + s * (STEP * q)

    def back_row(s, q):
        return (1 - s) * (HALF - BACK * (q + 1)) + s * (BACK * q)

    lane = lax.broadcasted_iota(jnp.int32, (CH, WIDTH), 1)

    def convolved(h):
        view = [xp[h + i] for i in range(4)]
        right = jnp.concatenate(
            [jnp.concatenate([view[i], view[i + 1]], axis=1) for i in range(3)], axis=0
        )
        return jnp.dot(wc[...], right, preferred_element_type=F32)

    def driven(acc, e):
        part = acc[:, e * WIDTH : (e + 1) * WIDTH]
        left = jnp.where(lane == 0, 0.0, pltpu.roll(part[0:CH], 1, 1))
        after = jnp.where(lane == WIDTH - 1, 0.0, pltpu.roll(part[2 * CH :], WIDTH - 1, 1))
        return coef[0] * (left + part[CH : 2 * CH] + after)

    def pair_copy(q):
        r = first_row(1 - core, q)
        return pltpu.make_async_remote_copy(
            src_ref=pair_out.at[pl.ds(r, STEP)], dst_ref=pair_in.at[pl.ds(r, STEP)],
            send_sem=pair_s, recv_sem=pair_r.at[q],
            device_id={"tm": partner}, device_id_type=MESH,
        )

    def pair_arrival(q):
        r = first_row(core, q)
        return pltpu.make_async_remote_copy(
            src_ref=pair_out.at[pl.ds(r, STEP)], dst_ref=pair_in.at[pl.ds(r, STEP)],
            send_sem=pair_s, recv_sem=pair_r.at[q],
            device_id={"tm": partner}, device_id_type=MESH,
        )

    def a_copy(d):
        to = peer(d)
        return pltpu.make_async_remote_copy(
            src_ref=coef.at[5, pl.ds(pl.multiple_of(to * BAND, BAND), BAND)],
            dst_ref=achip.at[chip],
            send_sem=a_s, recv_sem=a_r,
            device_id={"tm": to * 2 + core}, device_id_type=MESH,
        )

    def up_copy(q, d):
        to = peer(d)
        r = first_row(core, q)
        return pltpu.make_async_remote_copy(
            src_ref=merged.at[pl.ds(r, STEP), pl.ds(pl.multiple_of(to * BAND, BAND), BAND)],
            dst_ref=up_in.at[chip, pl.ds(r, STEP)],
            send_sem=up_s, recv_sem=up_r.at[q],
            device_id={"tm": to * 2 + core}, device_id_type=MESH,
        )

    def up_local(q):
        r = first_row(core, q)
        return pltpu.make_async_copy(
            merged.at[pl.ds(r, STEP), pl.ds(pl.multiple_of(chip * BAND, BAND), BAND)],
            up_in.at[chip, pl.ds(r, STEP)],
            up_r.at[q],
        )

    def down_copy(q, d):
        to = peer(d)
        r = back_row(core, q)
        return pltpu.make_async_remote_copy(
            src_ref=down_out.at[to, pl.ds(r, BACK)],
            dst_ref=entry.at[pl.ds(r, BACK), pl.ds(pl.multiple_of(chip * BAND, BAND), BAND)],
            send_sem=down_s, recv_sem=down_r.at[q],
            device_id={"tm": to * 2 + core}, device_id_type=MESH,
        )

    def down_local(q):
        r = back_row(core, q)
        return pltpu.make_async_copy(
            down_out.at[chip, pl.ds(r, BACK)],
            entry.at[pl.ds(r, BACK), pl.ds(pl.multiple_of(chip * BAND, BAND), BAND)],
            down_r.at[q],
        )

    def last_copy(q):
        r = back_row(core, q)
        return pltpu.make_async_remote_copy(
            src_ref=last_out.at[pl.ds(r, BACK)], dst_ref=last_in.at[pl.ds(r, BACK)],
            send_sem=last_s, recv_sem=last_r.at[q],
            device_id={"tm": partner}, device_id_type=MESH,
        )

    def last_arrival(q):
        r = back_row(1 - core, q)
        return pltpu.make_async_remote_copy(
            src_ref=last_out.at[pl.ds(r, BACK)], dst_ref=last_in.at[pl.ds(r, BACK)],
            send_sem=last_s, recv_sem=last_r.at[q],
            device_id={"tm": partner}, device_id_type=MESH,
        )

    def arrived(part, sem):
        pltpu.make_async_copy(part, part, sem).wait()

    def sent(part, sem):
        pltpu.make_async_copy(part, part, sem).wait()

    def each(n0, n1, body):
        def run(i, carry):
            body(i)
            return carry

        lax.fori_loop(n0, n1, run, 0)

    other = 1 - core
    second = core.astype(F32)

    def conv_tile(q, t):
        r = first_row(other, q) + 2 * t
        theirs = convolved(r + HALF * other)
        h = first_row(core, q) + 2 * t + HALF * core
        ours = convolved(h)
        for e in range(2):
            value = driven(theirs, e)
            drive[r + HALF * other + e] = value
            pair_out[r + e] = value.astype(BF16)
        for e in range(2):
            drive[h + e] = driven(ours, e)

    a_local = pltpu.make_async_copy(
        coef.at[5, pl.ds(pl.multiple_of(chip * BAND, BAND), BAND)], achip.at[chip], a_r
    )

    def coefficients():
        dec_copy.wait()
        mine = decs[0]
        theirs = column(lines[2])
        coef[1] = (1.0 - second) * theirs + second
        coef[2] = (1.0 - second) + second * mine
        coef[5] = mine * theirs
        coef[3] = (1.0 - second) * mine + second * (mine * theirs)

    def merge_half(q):
        pair_arrival(q).wait_recv()
        r0 = first_row(core, q)

        def merge(e):
            r = r0 + e
            own = drive[r + HALF * core]
            total = coef[1] * own + coef[2] * pair_in[r].astype(F32)
            merged[r] = total.astype(BF16)
            drive[r + HALF * core] = (1.0 - second) * own + second * total

        each(0, STEP, merge)
        each(1, CHIPS, lambda d: up_copy(q, d).start())
        up_local(q).start()

    def scan(q):
        arrived(up_in.at[:, pl.ds(first_row(core, q), STEP)], up_r.at[q])
        rows = pl.ds(first_row(core, q), STEP)
        state = jnp.zeros((STEP, BAND, WIDTH), F32)
        for i in range(CHIPS):
            down_out[i, rows] = state.astype(BF16)
            if i < CHIPS - 1:
                state = achip[i][None] * state + up_in[i, rows].astype(F32)

        def give(p):
            each(1, CHIPS, lambda d: down_copy(p, d).start())
            down_local(p).start()

        each(STEP // BACK * q, STEP // BACK * (q + 1), give)

    reorder(1)
    reorder(2)
    pltpu.make_async_copy(wc, wc, load_sem.at[5]).wait()
    each(0, STEP // 2, lambda t: conv_tile(0, t))
    pl.semaphore_wait(barrier, CHIPS + 2)
    dec_copy.start()
    pair_copy(0).start()

    def front(q):
        @pl.when(q == CHUNKS - 1)
        def _():
            halo(0).wait()
            halo(1).wait()

            @pl.when(sp == 0)
            def _():
                xp[0] = jnp.zeros((CH, WIDTH), BF16)

            @pl.when(sp == 3)
            def _():
                xp[ROWS + 1] = jnp.zeros((CH, WIDTH), BF16)

        def step(t):
            conv_tile(q, t)

            @pl.when((q == 1) & (t == 0))
            def _():
                coefficients()
                merge_half(0)
                each(1, CHIPS, lambda d: a_copy(d).start())
                a_local.start()

        each(0, STEP // 2, step)
        pair_copy(q).start()

        @pl.when(q == 1)
        def _():
            reorder(0)
            reorder(3)
            halo(0).start()
            halo(1).start()
            wo_load.wait()

        @pl.when(q > 1)
        def _():
            merge_half(q - 1)

    each(1, CHUNKS, front)
    arrived(achip, a_r)
    each(0, EARLY, scan)
    merge_half(CHUNKS - 1)
    each(EARLY, CHUNKS, scan)

    def project(h, memory):
        out = jnp.dot(
            wo[...], jnp.concatenate(memory, axis=1), preferred_element_type=F32
        )
        for e in range(2):
            row = h + e
            y_rows[row // GROUP, pl.ds(lax.rem(row, GROUP), CH, stride=GROUP), :] = (
                out[:, e * WIDTH : (e + 1) * WIDTH] + coef[4] * xp[row + 1].astype(F32)
            )

    def put(s, q):
        @pl.when(lax.rem(q, GROUP // BACK) == GROUP // BACK - 1)
        def _():
            b = (back_row(s, q) + HALF * s) // GROUP
            y_out[:, pl.ds(pl.multiple_of(b * GROUP, GROUP), GROUP)] = (
                y_rows[b].reshape(CH, GROUP, WIDTH).astype(BF16)
            )

    def finish_own(q):
        arrived(entry.at[pl.ds(back_row(core, q), BACK)], down_r.at[q])
        r0 = back_row(core, q)

        def answer(e):
            r = r0 + e
            enter = entry[r].astype(F32)
            memory = coef[3] * enter + drive[r + HALF * core]
            drive[r + HALF * core] = memory
            last_out[r] = ((1.0 - second) * memory + second * enter).astype(BF16)

        each(0, BACK, answer)
        last_copy(q).start()

        def tile(t):
            h = r0 + 2 * t + HALF * core
            project(h, [drive[h + e].astype(BF16) for e in range(2)])

        each(0, BACK // 2, tile)
        put(core, q)

    def finish_other(q):
        last_arrival(q).wait_recv()
        r0 = back_row(other, q)

        def tile(t):
            r = r0 + 2 * t
            h = r + HALF * other
            project(
                h,
                [
                    (decs[0] * last_in[r + e].astype(F32) + drive[h + e]).astype(BF16)
                    for e in range(2)
                ],
            )

        each(0, BACK // 2, tile)
        put(other, q)

    def finish(q):
        @pl.when(q < RETURNS)
        def _():
            finish_own(q)

        @pl.when(q > 0)
        def _():
            finish_other(q - 1)

    each(0, RETURNS + 1, finish)
    sent(pair_out, pair_s)
    sent(last_out, last_s)
    sent(achip.at[pl.ds(0, CHIPS - 1)], a_s)
    sent(up_in.at[pl.ds(0, CHIPS - 1)], up_s)
    sent(down_out.at[pl.ds(0, CHIPS - 1)], down_s)


def on_device(frames_in, conv_weight, out_weight, skip_gain, decays):
    rows = frames_in[0]
    pin = lambda a: pltpu.with_memory_space_constraint(a, pltpu.HBM)
    dma = pltpu.SemaphoreType.DMA
    y = pl.pallas_call(
        kernel,
        out_shape=jax.ShapeDtypeStruct((CH, ROWS, WIDTH), BF16),
        in_specs=[pl.BlockSpec(memory_space=pl.ANY)] * 5,
        out_specs=pl.BlockSpec(memory_space=pltpu.VMEM),
        scratch_shapes=[
            pltpu.VMEM((ROWS + 2, CH, WIDTH), BF16),
            pltpu.VMEM((3 * CH, 3 * CH), BF16),
            pltpu.VMEM((CH, CH), BF16),
            pltpu.VMEM((ROWS, CH, WIDTH), F32),
            pltpu.VMEM((6, CH, WIDTH), F32),
            pltpu.VMEM((1, CH, WIDTH), F32),
            pltpu.VMEM((CHIPS, BAND, WIDTH), F32),
            pltpu.VMEM((HALF, CH, WIDTH), BF16),
            pltpu.VMEM((HALF, CH, WIDTH), BF16),
            pltpu.VMEM((HALF, CH, WIDTH), BF16),
            pltpu.VMEM((CHIPS, HALF, BAND, WIDTH), BF16),
            pltpu.VMEM((CHIPS, HALF, BAND, WIDTH), BF16),
            pltpu.VMEM((HALF, CH, WIDTH), BF16),
            pltpu.VMEM((HALF, CH, WIDTH), BF16),
            pltpu.VMEM((HALF, CH, WIDTH), BF16),
            pltpu.VMEM((ROWS // GROUP, CH * GROUP, WIDTH), F32),
            pltpu.VMEM((ROWS // GROUP, CH, GROUP, WIDTH), BF16),
            pltpu.VMEM((CH * GROUP, WIDTH), F32),
            pltpu.VMEM((3, 1, CH), F32),
            dma((8,)),
            dma((2,)),
            dma((2,)),
            dma,
            dma,
            dma,
            dma,
            dma,
            dma((CHUNKS,)),
            dma,
            dma((CHUNKS,)),
            dma,
            dma((RETURNS,)),
            dma,
            dma((RETURNS,)),
        ],
        compiler_params=pltpu.CompilerParams(
            collective_id=0, has_side_effects=True, vmem_limit_bytes=VMEM_BYTES
        ),
    )(pin(rows), pin(conv_weight), pin(out_weight), pin(skip_gain[None, :]), pin(decays))
    return y[None]


def solution(mesh):
    placed = (P("tm", None, "space", None), P(), P(), P(), P("tm", None))
    return jax.shard_map(
        on_device,
        mesh=mesh,
        in_specs=placed,
        out_specs=P("tm", None, "space", None),
        check_vma=False,
    )
```

```python
import functools

import jax
import jax.numpy as jnp
from jax import lax
from jax.experimental import pallas as pl
from jax.experimental.pallas import tpu as pltpu
from jax.sharding import PartitionSpec as P

MESH = pl.DeviceIdType.MESH
ROWS = 32
HALF = 16
CH = 256
WIDTH = 128
CHIPS = 16
BAND = CH // CHIPS
CHUNKS = 8
GROUP = 8
EARLY = 0
VMEM_BYTES = 48 << 20
STEP = HALF // CHUNKS
RETURNS = 8
BACK = HALF // RETURNS
F32 = jnp.float32
BF16 = jnp.bfloat16


def column(row):
    return jnp.transpose(jnp.broadcast_to(row, (WIDTH, CH)), (1, 0))


def kernel(
    x_hbm, w_hbm, wo_hbm, skip_hbm, dec_hbm, y_out,
    xp, wc, wo, drive, coef, decs, achip, pair_out, pair_in, merged, up_in, down_out, entry,
    last_out, last_in, y_rows, raw, stage, lines,
    load_sem, halo_s, halo_r, dec_s, dec_r, a_s, a_r, pair_s, pair_r, up_s, up_r,
    down_s, down_r, last_s, last_r,
):
    tm = lax.axis_index("tm")
    sp = lax.axis_index("space")
    chip = tm // 2
    core = lax.rem(tm, 2)
    partner = chip * 2 + (1 - core)
    above = lax.rem(sp + 3, 4)
    below = lax.rem(sp + 1, 4)

    def peer(d):
        return lax.rem(chip + d, CHIPS)

    x_loads = [
        pltpu.make_async_copy(
            x_hbm.at[:, pl.ds(GROUP * b, GROUP)], raw.at[b], load_sem.at[b]
        )
        for b in range(ROWS // GROUP)
    ]
    small_loads = [
        pltpu.make_async_copy(dec_hbm, lines.at[0], load_sem.at[6]),
        pltpu.make_async_copy(skip_hbm, lines.at[1], load_sem.at[7]),
    ]
    for load in small_loads:
        load.start()
    x_loads[1].start()
    x_loads[2].start()
    loads = []
    for i in range(3):
        for j in range(3):
            loads.append(
                pltpu.make_async_copy(
                    w_hbm.at[i, j],
                    wc.at[pl.ds(j * CH, CH), pl.ds(i * CH, CH)],
                    load_sem.at[5],
                )
            )
    wo_load = pltpu.make_async_copy(wo_hbm, wo, load_sem.at[4])
    for load in loads:
        load.start()
    x_loads[0].start()
    x_loads[3].start()
    wo_load.start()

    barrier = pltpu.get_barrier_semaphore()

    def greet(d, carry):
        pl.semaphore_signal(
            barrier, inc=1, device_id={"tm": peer(d) * 2 + core}, device_id_type=MESH
        )
        return carry

    pl.semaphore_signal(barrier, inc=1, device_id={"tm": partner}, device_id_type=MESH)
    pl.semaphore_signal(barrier, inc=1, device_id={"space": above}, device_id_type=MESH)
    pl.semaphore_signal(barrier, inc=1, device_id={"space": below}, device_id_type=MESH)
    lax.fori_loop(1, CHIPS, greet, 0, unroll=True)

    for load in small_loads:
        load.wait()
    own_decay = column(lines[0])
    decs[0] = own_decay
    coef[0] = jnp.sqrt(1.0 - own_decay * own_decay)
    coef[4] = column(lines[1])

    def halo(side):
        row, slot, target = ((ROWS, 0, below), (1, ROWS + 1, above))[side]
        return pltpu.make_async_remote_copy(
            src_ref=xp.at[row], dst_ref=xp.at[slot], send_sem=halo_s.at[side],
            recv_sem=halo_r.at[side], device_id={"space": target}, device_id_type=MESH,
        )

    def reorder(b):
        x_loads[b].wait()
        stage[...] = raw[b].astype(F32).reshape(CH * GROUP, WIDTH)

        def row(r):
            xp[1 + GROUP * b + r] = stage[pl.ds(r, CH, stride=GROUP), :].astype(BF16)

        for r in range(GROUP):
            row(r)

    dec_copy = pltpu.make_async_remote_copy(
        src_ref=lines.at[0], dst_ref=lines.at[2], send_sem=dec_s, recv_sem=dec_r,
        device_id={"tm": partner}, device_id_type=MESH,
    )

    def first_row(s, q):
        return (1 - s) * (HALF - STEP * (q + 1)) + s * (STEP * q)

    def back_row(s, q):
        return (1 - s) * (HALF - BACK * (q + 1)) + s * (BACK * q)

    lane = lax.broadcasted_iota(jnp.int32, (CH, WIDTH), 1)

    def convolved(h):
        view = [xp[h + i] for i in range(4)]
        right = jnp.concatenate(
            [jnp.concatenate([view[i], view[i + 1]], axis=1) for i in range(3)], axis=0
        )
        return jnp.dot(wc[...], right, preferred_element_type=F32)

    def driven(acc, e):
        part = acc[:, e * WIDTH : (e + 1) * WIDTH]
        left = jnp.where(lane == 0, 0.0, pltpu.roll(part[0:CH], 1, 1))
        after = jnp.where(lane == WIDTH - 1, 0.0, pltpu.roll(part[2 * CH :], WIDTH - 1, 1))
        return coef[0] * (left + part[CH : 2 * CH] + after)

    def pair_copy(q):
        r = first_row(1 - core, q)
        return pltpu.make_async_remote_copy(
            src_ref=pair_out.at[pl.ds(r, STEP)], dst_ref=pair_in.at[pl.ds(r, STEP)],
            send_sem=pair_s, recv_sem=pair_r.at[q],
            device_id={"tm": partner}, device_id_type=MESH,
        )

    def pair_arrival(q):
        r = first_row(core, q)
        return pltpu.make_async_remote_copy(
            src_ref=pair_out.at[pl.ds(r, STEP)], dst_ref=pair_in.at[pl.ds(r, STEP)],
            send_sem=pair_s, recv_sem=pair_r.at[q],
            device_id={"tm": partner}, device_id_type=MESH,
        )

    def a_copy(d):
        to = peer(d)
        return pltpu.make_async_remote_copy(
            src_ref=coef.at[5, pl.ds(pl.multiple_of(to * BAND, BAND), BAND)],
            dst_ref=achip.at[chip],
            send_sem=a_s, recv_sem=a_r,
            device_id={"tm": to * 2 + core}, device_id_type=MESH,
        )

    def up_copy(q, d):
        to = peer(d)
        r = first_row(core, q)
        return pltpu.make_async_remote_copy(
            src_ref=merged.at[pl.ds(r, STEP), pl.ds(pl.multiple_of(to * BAND, BAND), BAND)],
            dst_ref=up_in.at[chip, pl.ds(r, STEP)],
            send_sem=up_s, recv_sem=up_r.at[q],
            device_id={"tm": to * 2 + core}, device_id_type=MESH,
        )

    def up_local(q):
        r = first_row(core, q)
        return pltpu.make_async_copy(
            merged.at[pl.ds(r, STEP), pl.ds(pl.multiple_of(chip * BAND, BAND), BAND)],
            up_in.at[chip, pl.ds(r, STEP)],
            up_r.at[q],
        )

    def down_copy(q, d):
        to = peer(d)
        r = back_row(core, q)
        return pltpu.make_async_remote_copy(
            src_ref=down_out.at[to, pl.ds(r, BACK)],
            dst_ref=entry.at[pl.ds(r, BACK), pl.ds(pl.multiple_of(chip * BAND, BAND), BAND)],
            send_sem=down_s, recv_sem=down_r.at[q],
            device_id={"tm": to * 2 + core}, device_id_type=MESH,
        )

    def down_local(q):
        r = back_row(core, q)
        return pltpu.make_async_copy(
            down_out.at[chip, pl.ds(r, BACK)],
            entry.at[pl.ds(r, BACK), pl.ds(pl.multiple_of(chip * BAND, BAND), BAND)],
            down_r.at[q],
        )

    def last_copy(q):
        r = back_row(core, q)
        return pltpu.make_async_remote_copy(
            src_ref=last_out.at[pl.ds(r, BACK)], dst_ref=last_in.at[pl.ds(r, BACK)],
            send_sem=last_s, recv_sem=last_r.at[q],
            device_id={"tm": partner}, device_id_type=MESH,
        )

    def last_arrival(q):
        r = back_row(1 - core, q)
        return pltpu.make_async_remote_copy(
            src_ref=last_out.at[pl.ds(r, BACK)], dst_ref=last_in.at[pl.ds(r, BACK)],
            send_sem=last_s, recv_sem=last_r.at[q],
            device_id={"tm": partner}, device_id_type=MESH,
        )

    def arrived(part, sem):
        pltpu.make_async_copy(part, part, sem).wait()

    def sent(part, sem):
        pltpu.make_async_copy(part, part, sem).wait()

    def each(n0, n1, body):
        def run(i, carry):
            body(i)
            return carry

        lax.fori_loop(n0, n1, run, 0)

    other = 1 - core
    second = core.astype(F32)

    def conv_tile(q, t):
        r = first_row(other, q) + 2 * t
        theirs = convolved(r + HALF * other)
        h = first_row(core, q) + 2 * t + HALF * core
        ours = convolved(h)
        for e in range(2):
            value = driven(theirs, e)
            drive[r + HALF * other + e] = value
            pair_out[r + e] = value.astype(BF16)
        for e in range(2):
            drive[h + e] = driven(ours, e)

    a_local = pltpu.make_async_copy(
        coef.at[5, pl.ds(pl.multiple_of(chip * BAND, BAND), BAND)], achip.at[chip], a_r
    )

    def coefficients():
        dec_copy.wait()
        mine = decs[0]
        theirs = column(lines[2])
        coef[1] = (1.0 - second) * theirs + second
        coef[2] = (1.0 - second) + second * mine
        coef[5] = mine * theirs
        coef[3] = (1.0 - second) * mine + second * (mine * theirs)

    def merge_half(q):
        pair_arrival(q).wait_recv()
        r0 = first_row(core, q)

        def merge(e):
            r = r0 + e
            own = drive[r + HALF * core]
            total = coef[1] * own + coef[2] * pair_in[r].astype(F32)
            merged[r] = total.astype(BF16)
            drive[r + HALF * core] = (1.0 - second) * own + second * total

        each(0, STEP, merge)
        for d in range(1, CHIPS):
            up_copy(q, d).start()
        up_local(q).start()

    def scan(q):
        arrived(up_in.at[:, pl.ds(first_row(core, q), STEP)], up_r.at[q])
        rows = pl.ds(first_row(core, q), STEP)
        state = jnp.zeros((STEP, BAND, WIDTH), F32)
        for i in range(CHIPS):
            down_out[i, rows] = state.astype(BF16)
            if i < CHIPS - 1:
                state = achip[i][None] * state + up_in[i, rows].astype(F32)

        def give(p):
            for d in range(1, CHIPS):
                down_copy(p, d).start()
            down_local(p).start()

        each(STEP // BACK * q, STEP // BACK * (q + 1), give)

    reorder(1)
    reorder(2)
    pltpu.make_async_copy(wc, wc, load_sem.at[5]).wait()
    each(0, STEP // 2, lambda t: conv_tile(0, t))
    pl.semaphore_wait(barrier, CHIPS + 2)
    dec_copy.start()
    pair_copy(0).start()

    def front(q):
        @pl.when(q == CHUNKS - 1)
        def _():
            halo(0).wait()
            halo(1).wait()

            @pl.when(sp == 0)
            def _():
                xp[0] = jnp.zeros((CH, WIDTH), BF16)

            @pl.when(sp == 3)
            def _():
                xp[ROWS + 1] = jnp.zeros((CH, WIDTH), BF16)

        def step(t):
            conv_tile(q, t)

            @pl.when((q == 1) & (t == 0))
            def _():
                coefficients()
                merge_half(0)
                each(1, CHIPS, lambda d: a_copy(d).start())
                a_local.start()

        each(0, STEP // 2, step)
        pair_copy(q).start()

        @pl.when(q == 1)
        def _():
            reorder(0)
            reorder(3)
            halo(0).start()
            halo(1).start()
            wo_load.wait()

        @pl.when(q > 1)
        def _():
            merge_half(q - 1)

    each(1, CHUNKS, front)
    arrived(achip, a_r)
    each(0, EARLY, scan)
    merge_half(CHUNKS - 1)
    each(EARLY, CHUNKS, scan)

    def project(h, memory):
        out = jnp.dot(
            wo[...], jnp.concatenate(memory, axis=1), preferred_element_type=F32
        )
        for e in range(2):
            row = h + e
            y_rows[row // GROUP, pl.ds(lax.rem(row, GROUP), CH, stride=GROUP), :] = (
                out[:, e * WIDTH : (e + 1) * WIDTH] + coef[4] * xp[row + 1].astype(F32)
            )

    def put(s, q):
        @pl.when(lax.rem(q, GROUP // BACK) == GROUP // BACK - 1)
        def _():
            b = (back_row(s, q) + HALF * s) // GROUP
            y_out[:, pl.ds(pl.multiple_of(b * GROUP, GROUP), GROUP)] = (
                y_rows[b].reshape(CH, GROUP, WIDTH).astype(BF16)
            )

    def finish_own(q):
        arrived(entry.at[pl.ds(back_row(core, q), BACK)], down_r.at[q])
        r0 = back_row(core, q)

        def answer(e):
            r = r0 + e
            enter = entry[r].astype(F32)
            memory = coef[3] * enter + drive[r + HALF * core]
            drive[r + HALF * core] = memory
            last_out[r] = ((1.0 - second) * memory + second * enter).astype(BF16)

        each(0, BACK, answer)
        last_copy(q).start()

        def tile(t):
            h = r0 + 2 * t + HALF * core
            project(h, [drive[h + e].astype(BF16) for e in range(2)])

        each(0, BACK // 2, tile)
        put(core, q)

    def finish_other(q):
        last_arrival(q).wait_recv()
        r0 = back_row(other, q)

        def tile(t):
            r = r0 + 2 * t
            h = r + HALF * other
            project(
                h,
                [
                    (decs[0] * last_in[r + e].astype(F32) + drive[h + e]).astype(BF16)
                    for e in range(2)
                ],
            )

        each(0, BACK // 2, tile)
        put(other, q)

    def finish(q):
        @pl.when(q < RETURNS)
        def _():
            finish_own(q)

        @pl.when(q > 0)
        def _():
            finish_other(q - 1)

    each(0, RETURNS + 1, finish)
    sent(pair_out, pair_s)
    sent(last_out, last_s)
    sent(achip.at[pl.ds(0, CHIPS - 1)], a_s)
    sent(up_in.at[pl.ds(0, CHIPS - 1)], up_s)
    sent(down_out.at[pl.ds(0, CHIPS - 1)], down_s)


def on_device(frames_in, conv_weight, out_weight, skip_gain, decays):
    rows = frames_in[0]
    pin = lambda a: pltpu.with_memory_space_constraint(a, pltpu.HBM)
    dma = pltpu.SemaphoreType.DMA
    y = pl.pallas_call(
        kernel,
        out_shape=jax.ShapeDtypeStruct((CH, ROWS, WIDTH), BF16),
        in_specs=[pl.BlockSpec(memory_space=pl.ANY)] * 5,
        out_specs=pl.BlockSpec(memory_space=pltpu.VMEM),
        scratch_shapes=[
            pltpu.VMEM((ROWS + 2, CH, WIDTH), BF16),
            pltpu.VMEM((3 * CH, 3 * CH), BF16),
            pltpu.VMEM((CH, CH), BF16),
            pltpu.VMEM((ROWS, CH, WIDTH), F32),
            pltpu.VMEM((6, CH, WIDTH), F32),
            pltpu.VMEM((1, CH, WIDTH), F32),
            pltpu.VMEM((CHIPS, BAND, WIDTH), F32),
            pltpu.VMEM((HALF, CH, WIDTH), BF16),
            pltpu.VMEM((HALF, CH, WIDTH), BF16),
            pltpu.VMEM((HALF, CH, WIDTH), BF16),
            pltpu.VMEM((CHIPS, HALF, BAND, WIDTH), BF16),
            pltpu.VMEM((CHIPS, HALF, BAND, WIDTH), BF16),
            pltpu.VMEM((HALF, CH, WIDTH), BF16),
            pltpu.VMEM((HALF, CH, WIDTH), BF16),
            pltpu.VMEM((HALF, CH, WIDTH), BF16),
            pltpu.VMEM((ROWS // GROUP, CH * GROUP, WIDTH), F32),
            pltpu.VMEM((ROWS // GROUP, CH, GROUP, WIDTH), BF16),
            pltpu.VMEM((CH * GROUP, WIDTH), F32),
            pltpu.VMEM((3, 1, CH), F32),
            dma((8,)),
            dma((2,)),
            dma((2,)),
            dma,
            dma,
            dma,
            dma,
            dma,
            dma((CHUNKS,)),
            dma,
            dma((CHUNKS,)),
            dma,
            dma((RETURNS,)),
            dma,
            dma((RETURNS,)),
        ],
        compiler_params=pltpu.CompilerParams(
            collective_id=0, has_side_effects=True, vmem_limit_bytes=VMEM_BYTES
        ),
    )(pin(rows), pin(conv_weight), pin(out_weight), pin(skip_gain[None, :]), pin(decays))
    return y[None]


def solution(mesh):
    placed = (P("tm", None, "space", None), P(), P(), P(), P("tm", None))
    return jax.shard_map(
        on_device,
        mesh=mesh,
        in_specs=placed,
        out_specs=P("tm", None, "space", None),
        check_vma=False,
    )
```

```python
import functools

import jax
import jax.numpy as jnp
from jax import lax
from jax.experimental import pallas as pl
from jax.experimental.pallas import tpu as pltpu
from jax.sharding import PartitionSpec as P

MESH = pl.DeviceIdType.MESH
ROWS = 32
HALF = 16
CH = 256
WIDTH = 128
CHIPS = 16
BAND = CH // CHIPS
CHUNKS = 8
GROUP = 8
EARLY = 1
VMEM_BYTES = 48 << 20
STEP = HALF // CHUNKS
RETURNS = 8
BACK = HALF // RETURNS
F32 = jnp.float32
BF16 = jnp.bfloat16


def column(row):
    return jnp.transpose(jnp.broadcast_to(row, (WIDTH, CH)), (1, 0))


def kernel(
    x_hbm, w_hbm, wo_hbm, skip_hbm, dec_hbm, y_out,
    xp, wc, wo, drive, coef, decs, achip, pair_out, pair_in, merged, up_in, down_out, entry,
    last_out, last_in, y_rows, raw, stage, lines,
    load_sem, halo_s, halo_r, dec_s, dec_r, a_s, a_r, pair_s, pair_r, up_s, up_r,
    down_s, down_r, last_s, last_r,
):
    tm = lax.axis_index("tm")
    sp = lax.axis_index("space")
    chip = tm // 2
    core = lax.rem(tm, 2)
    partner = chip * 2 + (1 - core)
    above = lax.rem(sp + 3, 4)
    below = lax.rem(sp + 1, 4)

    def peer(d):
        return lax.rem(chip + d, CHIPS)

    x_loads = [
        pltpu.make_async_copy(
            x_hbm.at[:, pl.ds(GROUP * b, GROUP)], raw.at[b], load_sem.at[b]
        )
        for b in range(ROWS // GROUP)
    ]
    small_loads = [
        pltpu.make_async_copy(dec_hbm, lines.at[0], load_sem.at[6]),
        pltpu.make_async_copy(skip_hbm, lines.at[1], load_sem.at[7]),
    ]
    for load in small_loads:
        load.start()
    x_loads[1].start()
    x_loads[2].start()
    loads = []
    for i in range(3):
        for j in range(3):
            loads.append(
                pltpu.make_async_copy(
                    w_hbm.at[i, j],
                    wc.at[pl.ds(j * CH, CH), pl.ds(i * CH, CH)],
                    load_sem.at[5],
                )
            )
    wo_load = pltpu.make_async_copy(wo_hbm, wo, load_sem.at[4])
    for load in loads:
        load.start()
    x_loads[0].start()
    x_loads[3].start()
    wo_load.start()

    barrier = pltpu.get_barrier_semaphore()

    def greet(d, carry):
        pl.semaphore_signal(
            barrier, inc=1, device_id={"tm": peer(d) * 2 + core}, device_id_type=MESH
        )
        return carry

    pl.semaphore_signal(barrier, inc=1, device_id={"tm": partner}, device_id_type=MESH)
    pl.semaphore_signal(barrier, inc=1, device_id={"space": above}, device_id_type=MESH)
    pl.semaphore_signal(barrier, inc=1, device_id={"space": below}, device_id_type=MESH)
    lax.fori_loop(1, CHIPS, greet, 0, unroll=True)

    for load in small_loads:
        load.wait()
    own_decay = column(lines[0])
    decs[0] = own_decay
    coef[0] = jnp.sqrt(1.0 - own_decay * own_decay)
    coef[4] = column(lines[1])

    def halo(side):
        row, slot, target = ((ROWS, 0, below), (1, ROWS + 1, above))[side]
        return pltpu.make_async_remote_copy(
            src_ref=xp.at[row], dst_ref=xp.at[slot], send_sem=halo_s.at[side],
            recv_sem=halo_r.at[side], device_id={"space": target}, device_id_type=MESH,
        )

    def reorder(b):
        x_loads[b].wait()
        stage[...] = raw[b].astype(F32).reshape(CH * GROUP, WIDTH)

        def row(r):
            xp[1 + GROUP * b + r] = stage[pl.ds(r, CH, stride=GROUP), :].astype(BF16)

        for r in range(GROUP):
            row(r)

    dec_copy = pltpu.make_async_remote_copy(
        src_ref=lines.at[0], dst_ref=lines.at[2], send_sem=dec_s, recv_sem=dec_r,
        device_id={"tm": partner}, device_id_type=MESH,
    )

    def first_row(s, q):
        return (1 - s) * (HALF - STEP * (q + 1)) + s * (STEP * q)

    def back_row(s, q):
        return (1 - s) * (HALF - BACK * (q + 1)) + s * (BACK * q)

    lane = lax.broadcasted_iota(jnp.int32, (CH, WIDTH), 1)

    def convolved(h):
        view = [xp[h + i] for i in range(4)]
        right = jnp.concatenate(
            [jnp.concatenate([view[i], view[i + 1]], axis=1) for i in range(3)], axis=0
        )
        return jnp.dot(wc[...], right, preferred_element_type=F32)

    def driven(acc, e):
        part = acc[:, e * WIDTH : (e + 1) * WIDTH]
        left = jnp.where(lane == 0, 0.0, pltpu.roll(part[0:CH], 1, 1))
        after = jnp.where(lane == WIDTH - 1, 0.0, pltpu.roll(part[2 * CH :], WIDTH - 1, 1))
        return coef[0] * (left + part[CH : 2 * CH] + after)

    def pair_copy(q):
        r = first_row(1 - core, q)
        return pltpu.make_async_remote_copy(
            src_ref=pair_out.at[pl.ds(r, STEP)], dst_ref=pair_in.at[pl.ds(r, STEP)],
            send_sem=pair_s, recv_sem=pair_r.at[q],
            device_id={"tm": partner}, device_id_type=MESH,
        )

    def pair_arrival(q):
        r = first_row(core, q)
        return pltpu.make_async_remote_copy(
            src_ref=pair_out.at[pl.ds(r, STEP)], dst_ref=pair_in.at[pl.ds(r, STEP)],
            send_sem=pair_s, recv_sem=pair_r.at[q],
            device_id={"tm": partner}, device_id_type=MESH,
        )

    def a_copy(d):
        to = peer(d)
        return pltpu.make_async_remote_copy(
            src_ref=coef.at[5, pl.ds(pl.multiple_of(to * BAND, BAND), BAND)],
            dst_ref=achip.at[chip],
            send_sem=a_s, recv_sem=a_r,
            device_id={"tm": to * 2 + core}, device_id_type=MESH,
        )

    def up_copy(q, d):
        to = peer(d)
        r = first_row(core, q)
        return pltpu.make_async_remote_copy(
            src_ref=merged.at[pl.ds(r, STEP), pl.ds(pl.multiple_of(to * BAND, BAND), BAND)],
            dst_ref=up_in.at[chip, pl.ds(r, STEP)],
            send_sem=up_s, recv_sem=up_r.at[q],
            device_id={"tm": to * 2 + core}, device_id_type=MESH,
        )

    def up_local(q):
        r = first_row(core, q)
        return pltpu.make_async_copy(
            merged.at[pl.ds(r, STEP), pl.ds(pl.multiple_of(chip * BAND, BAND), BAND)],
            up_in.at[chip, pl.ds(r, STEP)],
            up_r.at[q],
        )

    def down_copy(q, d):
        to = peer(d)
        r = back_row(core, q)
        return pltpu.make_async_remote_copy(
            src_ref=down_out.at[to, pl.ds(r, BACK)],
            dst_ref=entry.at[pl.ds(r, BACK), pl.ds(pl.multiple_of(chip * BAND, BAND), BAND)],
            send_sem=down_s, recv_sem=down_r.at[q],
            device_id={"tm": to * 2 + core}, device_id_type=MESH,
        )

    def down_local(q):
        r = back_row(core, q)
        return pltpu.make_async_copy(
            down_out.at[chip, pl.ds(r, BACK)],
            entry.at[pl.ds(r, BACK), pl.ds(pl.multiple_of(chip * BAND, BAND), BAND)],
            down_r.at[q],
        )

    def last_copy(q):
        r = back_row(core, q)
        return pltpu.make_async_remote_copy(
            src_ref=last_out.at[pl.ds(r, BACK)], dst_ref=last_in.at[pl.ds(r, BACK)],
            send_sem=last_s, recv_sem=last_r.at[q],
            device_id={"tm": partner}, device_id_type=MESH,
        )

    def last_arrival(q):
        r = back_row(1 - core, q)
        return pltpu.make_async_remote_copy(
            src_ref=last_out.at[pl.ds(r, BACK)], dst_ref=last_in.at[pl.ds(r, BACK)],
            send_sem=last_s, recv_sem=last_r.at[q],
            device_id={"tm": partner}, device_id_type=MESH,
        )

    def arrived(part, sem):
        pltpu.make_async_copy(part, part, sem).wait()

    def sent(part, sem):
        pltpu.make_async_copy(part, part, sem).wait()

    def each(n0, n1, body):
        def run(i, carry):
            body(i)
            return carry

        lax.fori_loop(n0, n1, run, 0)

    other = 1 - core
    second = core.astype(F32)

    def conv_tile(q, t):
        r = first_row(other, q) + 2 * t
        theirs = convolved(r + HALF * other)
        h = first_row(core, q) + 2 * t + HALF * core
        ours = convolved(h)
        for e in range(2):
            value = driven(theirs, e)
            drive[r + HALF * other + e] = value
            pair_out[r + e] = value.astype(BF16)
        for e in range(2):
            drive[h + e] = driven(ours, e)

    a_local = pltpu.make_async_copy(
        coef.at[5, pl.ds(pl.multiple_of(chip * BAND, BAND), BAND)], achip.at[chip], a_r
    )

    def coefficients():
        dec_copy.wait()
        mine = decs[0]
        theirs = column(lines[2])
        coef[1] = (1.0 - second) * theirs + second
        coef[2] = (1.0 - second) + second * mine
        coef[5] = mine * theirs
        coef[3] = (1.0 - second) * mine + second * (mine * theirs)

    def merge_half(q):
        pair_arrival(q).wait_recv()
        r0 = first_row(core, q)

        def merge(e):
            r = r0 + e
            own = drive[r + HALF * core]
            total = coef[1] * own + coef[2] * pair_in[r].astype(F32)
            merged[r] = total.astype(BF16)
            drive[r + HALF * core] = (1.0 - second) * own + second * total

        each(0, STEP, merge)
        for d in range(1, CHIPS):
            up_copy(q, d).start()
        up_local(q).start()

    def scan(q):
        arrived(up_in.at[:, pl.ds(first_row(core, q), STEP)], up_r.at[q])
        rows = pl.ds(first_row(core, q), STEP)
        state = jnp.zeros((STEP, BAND, WIDTH), F32)
        for i in range(CHIPS):
            down_out[i, rows] = state.astype(BF16)
            if i < CHIPS - 1:
                state = achip[i][None] * state + up_in[i, rows].astype(F32)

        def give(p):
            for d in range(1, CHIPS):
                down_copy(p, d).start()
            down_local(p).start()

        each(STEP // BACK * q, STEP // BACK * (q + 1), give)

    reorder(1)
    reorder(2)
    pltpu.make_async_copy(wc, wc, load_sem.at[5]).wait()
    each(0, STEP // 2, lambda t: conv_tile(0, t))
    pl.semaphore_wait(barrier, CHIPS + 2)
    dec_copy.start()
    pair_copy(0).start()

    def front(q):
        @pl.when(q == CHUNKS - 1)
        def _():
            halo(0).wait()
            halo(1).wait()

            @pl.when(sp == 0)
            def _():
                xp[0] = jnp.zeros((CH, WIDTH), BF16)

            @pl.when(sp == 3)
            def _():
                xp[ROWS + 1] = jnp.zeros((CH, WIDTH), BF16)

        def step(t):
            conv_tile(q, t)

            @pl.when((q == 1) & (t == 0))
            def _():
                coefficients()
                merge_half(0)
                each(1, CHIPS, lambda d: a_copy(d).start())
                a_local.start()

        each(0, STEP // 2, step)
        pair_copy(q).start()

        @pl.when(q == 1)
        def _():
            reorder(0)
            reorder(3)
            halo(0).start()
            halo(1).start()
            wo_load.wait()

        @pl.when(q > 1)
        def _():
            merge_half(q - 1)

    each(1, CHUNKS, front)
    arrived(achip, a_r)
    each(0, EARLY, scan)
    merge_half(CHUNKS - 1)
    each(EARLY, CHUNKS, scan)

    def project(h, memory):
        out = jnp.dot(
            wo[...], jnp.concatenate(memory, axis=1), preferred_element_type=F32
        )
        for e in range(2):
            row = h + e
            y_rows[row // GROUP, pl.ds(lax.rem(row, GROUP), CH, stride=GROUP), :] = (
                out[:, e * WIDTH : (e + 1) * WIDTH] + coef[4] * xp[row + 1].astype(F32)
            )

    def put(s, q):
        @pl.when(lax.rem(q, GROUP // BACK) == GROUP // BACK - 1)
        def _():
            b = (back_row(s, q) + HALF * s) // GROUP
            y_out[:, pl.ds(pl.multiple_of(b * GROUP, GROUP), GROUP)] = (
                y_rows[b].reshape(CH, GROUP, WIDTH).astype(BF16)
            )

    def finish_own(q):
        arrived(entry.at[pl.ds(back_row(core, q), BACK)], down_r.at[q])
        r0 = back_row(core, q)

        def answer(e):
            r = r0 + e
            enter = entry[r].astype(F32)
            memory = coef[3] * enter + drive[r + HALF * core]
            drive[r + HALF * core] = memory
            last_out[r] = ((1.0 - second) * memory + second * enter).astype(BF16)

        each(0, BACK, answer)
        last_copy(q).start()

        def tile(t):
            h = r0 + 2 * t + HALF * core
            project(h, [drive[h + e].astype(BF16) for e in range(2)])

        each(0, BACK // 2, tile)
        put(core, q)

    def finish_other(q):
        last_arrival(q).wait_recv()
        r0 = back_row(other, q)

        def tile(t):
            r = r0 + 2 * t
            h = r + HALF * other
            project(
                h,
                [
                    (decs[0] * last_in[r + e].astype(F32) + drive[h + e]).astype(BF16)
                    for e in range(2)
                ],
            )

        each(0, BACK // 2, tile)
        put(other, q)

    def finish(q):
        @pl.when(q < RETURNS)
        def _():
            finish_own(q)

        @pl.when(q > 0)
        def _():
            finish_other(q - 1)

    each(0, RETURNS + 1, finish)
    sent(pair_out, pair_s)
    sent(last_out, last_s)
    sent(achip.at[pl.ds(0, CHIPS - 1)], a_s)
    sent(up_in.at[pl.ds(0, CHIPS - 1)], up_s)
    sent(down_out.at[pl.ds(0, CHIPS - 1)], down_s)


def on_device(frames_in, conv_weight, out_weight, skip_gain, decays):
    rows = frames_in[0]
    pin = lambda a: pltpu.with_memory_space_constraint(a, pltpu.HBM)
    dma = pltpu.SemaphoreType.DMA
    y = pl.pallas_call(
        kernel,
        out_shape=jax.ShapeDtypeStruct((CH, ROWS, WIDTH), BF16),
        in_specs=[pl.BlockSpec(memory_space=pl.ANY)] * 5,
        out_specs=pl.BlockSpec(memory_space=pltpu.VMEM),
        scratch_shapes=[
            pltpu.VMEM((ROWS + 2, CH, WIDTH), BF16),
            pltpu.VMEM((3 * CH, 3 * CH), BF16),
            pltpu.VMEM((CH, CH), BF16),
            pltpu.VMEM((ROWS, CH, WIDTH), F32),
            pltpu.VMEM((6, CH, WIDTH), F32),
            pltpu.VMEM((1, CH, WIDTH), F32),
            pltpu.VMEM((CHIPS, BAND, WIDTH), F32),
            pltpu.VMEM((HALF, CH, WIDTH), BF16),
            pltpu.VMEM((HALF, CH, WIDTH), BF16),
            pltpu.VMEM((HALF, CH, WIDTH), BF16),
            pltpu.VMEM((CHIPS, HALF, BAND, WIDTH), BF16),
            pltpu.VMEM((CHIPS, HALF, BAND, WIDTH), BF16),
            pltpu.VMEM((HALF, CH, WIDTH), BF16),
            pltpu.VMEM((HALF, CH, WIDTH), BF16),
            pltpu.VMEM((HALF, CH, WIDTH), BF16),
            pltpu.VMEM((ROWS // GROUP, CH * GROUP, WIDTH), F32),
            pltpu.VMEM((ROWS // GROUP, CH, GROUP, WIDTH), BF16),
            pltpu.VMEM((CH * GROUP, WIDTH), F32),
            pltpu.VMEM((3, 1, CH), F32),
            dma((8,)),
            dma((2,)),
            dma((2,)),
            dma,
            dma,
            dma,
            dma,
            dma,
            dma((CHUNKS,)),
            dma,
            dma((CHUNKS,)),
            dma,
            dma((RETURNS,)),
            dma,
            dma((RETURNS,)),
        ],
        compiler_params=pltpu.CompilerParams(
            collective_id=0, has_side_effects=True, vmem_limit_bytes=VMEM_BYTES
        ),
    )(pin(rows), pin(conv_weight), pin(out_weight), pin(skip_gain[None, :]), pin(decays))
    return y[None]


def solution(mesh):
    placed = (P("tm", None, "space", None), P(), P(), P(), P("tm", None))
    return jax.shard_map(
        on_device,
        mesh=mesh,
        in_specs=placed,
        out_specs=P("tm", None, "space", None),
        check_vma=False,
    )
```
